256 devices in a mesh: gx: 8 (over z_hi, y), gy: 4 (over z_lo), gz: 8 (over x, core).
Axes of the slice: x: 4, y: 4, z: 8 (z_hi: 2, z_lo: 4; z = z_hi * 4 + z_lo), core: 2. Of those that a mesh axis runs over, the one named last changes fastest.
Arguments:
- displacement: float32 [3, 32, 128, 2048], P(None, 'gx', 'gy', 'gz'), may hold values from -13 to 13
- density: float32 [32, 128, 2048], P('gx', 'gy', 'gz'), may hold values from 0.05 to 1
- material: int32 [32, 128, 2048], P('gx', 'gy', 'gz'), may hold values from 0 to 2
- fixed_mask: int32 [32, 128, 2048], P('gx', 'gy', 'gz'), may hold values 0 or 1
Outputs:
- adjoint: float32 [3, 32, 128, 2048], P(None, 'gx', 'gy', 'gz')
- sensitivity: float32 [32, 128, 2048], P('gx', 'gy', 'gz')
The draws below stay inside these ranges and needn't reach their ends.
All inputs are finite; a program needn't handle non-finite values. No bound on the sum of `fixed_mask` on one device may be relied on, other than what follows from the above.
Results may differ from the reference program's by a relative error of at most 0.000033.
Values sent between devices are 32-bit elements; how exact they have to be, the bound alone decides.
A program may use at most 64 MiB of HBM per device.

```python
import math
import jax
import jax.numpy as jnp
from jax import lax

CX = 4
NX = 32
NY = 128
NZ = 2048
NE = 8388608
N_GX = 8


def draw_displacement(key, part):
    key_base = jax.random.fold_in(key, 11)
    key_rough = jax.random.fold_in(key, 23)
    coord_x = jnp.arange(NX, dtype=jnp.float32) / max(NX - 1, 1)
    coord_y = jnp.arange(NY, dtype=jnp.float32) / max(NY - 1, 1)
    coord_z = jnp.arange(NZ, dtype=jnp.float32) / max(NZ - 1, 1)
    base = jnp.clip(jax.random.normal(key_base, (3, NX, NY, NZ), jnp.float32), -4.0, 4.0)
    rate = math.log(3.0) / 8.0
    rough = jnp.exp(jax.random.uniform(key_rough, (1, NX, NY, NZ), jnp.float32, -math.log(2.0), math.log(2.0)))
    ramp = jnp.exp(rate * (coord_x[:, None, None] + coord_y[None, :, None] + coord_z[None, None, :]))
    return (base * rough * ramp[None]).astype(jnp.float32)


def touch_ends(entries, stream_key, smallest, top_value):
    dims = entries.shape
    spot = [jax.random.randint(jax.random.fold_in(stream_key, axis), (), 0, dims[axis]) for axis in range(len(dims))]
    entries = entries.at[tuple(spot)].set(smallest)
    longest = dims.index(max(dims))
    spot[longest] = (spot[longest] + 1) % dims[longest]
    return entries.at[tuple(spot)].set(top_value)


def block_levels(rng, extent, shards, low, largest):
    factor_of, own = 1.0, jax.random.fold_in(rng, 6)
    for position, parts in shards:
        heights = jnp.exp(jax.random.uniform(jax.random.fold_in(own, position), (parts,), jnp.float32, low / len(shards), largest / len(shards)))
        factor_of = factor_of * jnp.repeat(heights, extent[position] // parts).reshape([-1 if axis == position else 1 for axis in range(len(extent))])
    return factor_of


def setup_inputs(seed: int = 0) -> dict:
    arg_keys = jax.random.split(jax.random.key(seed), 5)
    return {
        "displacement": draw_displacement(jax.random.fold_in(arg_keys[4], 71), 0),
        "density": jnp.clip(0.05 + 0.95 * jax.random.uniform(arg_keys[1], (NX, NY, NZ), jnp.float32) ** block_levels(arg_keys[1], (NX, NY, NZ), ((0, 8), (1, 4), (2, 8)), -0.2, 0.2), 0.05, 1.0),
        "material": touch_ends(jax.random.randint(arg_keys[2], (NX, NY, NZ), 0, 3), jax.random.fold_in(arg_keys[2], 1), 0, 2).astype(jnp.int32),
        "fixed_mask": touch_ends((jax.random.randint(arg_keys[3], (NX, NY, NZ), 0, 8) < 1).astype(jnp.int32), jax.random.fold_in(arg_keys[3], 1), 0, 1),
    }


lame_first = 0.577
lame_shear = 0.385
relax_weight = 0.6
tiny_shift = 1e-06
diag_scale = (0.577 + 4.0 * 0.385) / 16.0

def pair_sum(values, which_axis):
    length = values.shape[which_axis]
    return lax.slice_in_dim(values, 1, length, axis=which_axis) + lax.slice_in_dim(values, 0, length - 1, axis=which_axis)

def differ(values, which_axis):
    length = values.shape[which_axis]
    return lax.slice_in_dim(values, 1, length, axis=which_axis) - lax.slice_in_dim(values, 0, length - 1, axis=which_axis)

def along_x(values):
    return 0.25 * pair_sum(pair_sum(differ(values, -3), -2), -1)

def along_y(values):
    return 0.25 * pair_sum(pair_sum(differ(values, -2), -3), -1)

def along_z(values):
    return 0.25 * pair_sum(pair_sum(differ(values, -1), -3), -2)

def strains(nodal_field):
    grad_x = along_x(nodal_field)
    grad_y = along_y(nodal_field)
    grad_z = along_z(nodal_field)
    return jnp.stack([grad_x[0], grad_y[1], grad_z[2], grad_y[0] + grad_x[1], grad_z[1] + grad_y[2], grad_x[2] + grad_z[0]])

def stiffen(vector):
    trace_sum = vector[0] + vector[1] + vector[2]
    return jnp.stack([lame_first * trace_sum + 2.0 * lame_shear * vector[0], lame_first * trace_sum + 2.0 * lame_shear * vector[1], lame_first * trace_sum + 2.0 * lame_shear * vector[2], lame_shear * vector[3], lame_shear * vector[4], lame_shear * vector[5]])

def mises_quad(stress):
    return stress[0] ** 2 + stress[1] ** 2 + stress[2] ** 2 - stress[0] * stress[1] - stress[1] * stress[2] - stress[2] * stress[0] + 3.0 * (stress[3] ** 2 + stress[4] ** 2 + stress[5] ** 2)

def mises_slope(stress):
    return jnp.stack([2.0 * stress[0] - stress[1] - stress[2], 2.0 * stress[1] - stress[0] - stress[2], 2.0 * stress[2] - stress[0] - stress[1], 6.0 * stress[3], 6.0 * stress[4], 6.0 * stress[5]])

def forces(dual_stress):
    part_x = along_x(jnp.stack([dual_stress[0], dual_stress[3], dual_stress[5]]))
    part_y = along_y(jnp.stack([dual_stress[3], dual_stress[1], dual_stress[4]]))
    part_z = along_z(jnp.stack([dual_stress[5], dual_stress[4], dual_stress[2]]))
    return -(part_x + part_y + part_z)

def node_weight(stiffness):
    return diag_scale * pair_sum(pair_sum(pair_sum(stiffness, -3), -2), -1)

def factors(density, material):
    design = material == 1
    solid = material == 2
    root = jnp.sqrt(density)
    stiffness = 0.001 + jnp.where(design, density ** 3, jnp.where(solid, 1.0, 0.0))
    stress_factor = jnp.where(design, root, jnp.where(solid, 1.0, 0.0))
    stiff_slope = jnp.where(design, 3.0 * density ** 2, 0.0)
    stress_slope = jnp.where(design, 0.5 / root, 0.0)
    return (stiffness, stress_factor, stiff_slope, stress_slope)

def padded(values):
    if values.ndim == 4:
        return jnp.pad(values, ((0, 0), (1, 1), (1, 1), (1, 1)))
    return jnp.pad(values, 1)

def join_slabs(blocks):
    if blocks.ndim == 5:
        return jnp.moveaxis(blocks, 0, 1).reshape(blocks.shape[1], NX, NY, NZ)
    return blocks.reshape(NX, NY, NZ)

def reference(displacement, density, material, fixed_mask):
    stiffness, stress_factor, stiff_slope, stress_slope = factors(density, material)
    free_nodes = 1.0 - fixed_mask.astype(jnp.float32)
    nodal_pad = padded(displacement)
    stiff_pad = padded(stiffness)
    stress_pad = padded(stress_factor)
    zero_index = jnp.zeros((), jnp.int32)
    one_index = jnp.ones((), jnp.int32)
    starts = jnp.arange(N_GX, dtype=jnp.int32) * CX

    def element_part(start_row):
        nodal_field = lax.dynamic_slice(nodal_pad, (zero_index, start_row, zero_index, zero_index), (3, CX + 2, NY + 2, NZ + 2))
        elem_stiff = lax.dynamic_slice(stiff_pad, (start_row, zero_index, zero_index), (CX + 1, NY + 1, NZ + 1))
        elem_stress = lax.dynamic_slice(stress_pad, (start_row, zero_index, zero_index), (CX + 1, NY + 1, NZ + 1))
        unit_stress = stiffen(strains(nodal_field))
        unit_mises = mises_quad(unit_stress)
        mises_square = elem_stress ** 2 * unit_mises
        return (unit_stress, unit_mises, mises_square, elem_stiff, elem_stress)

    def power_part(start_row):
        return jnp.sum(element_part(start_row)[2][1:, 1:, 1:] ** 4)
    global_sum = jnp.sum(lax.map(power_part, starts))
    factor = (global_sum / NE + tiny_shift) ** (-0.875)

    def load_part(start_row):
        unit_stress, unit_mises, mises_square, elem_stiff, elem_stress = element_part(start_row)
        weight = factor * mises_square ** 3
        dual_stress = stiffen(0.5 * weight * elem_stress ** 2 * mises_slope(unit_stress))
        free_block = lax.dynamic_slice(free_nodes, (start_row, zero_index, zero_index), (CX, NY, NZ))
        return (forces(dual_stress), node_weight(elem_stiff) + (1.0 - free_block))
    load_blocks, diag_blocks = lax.map(load_part, starts)
    load_field = join_slabs(load_blocks)
    diagonal = join_slabs(diag_blocks)
    first_sweep = free_nodes * load_field / diagonal
    first_pad = padded(first_sweep)

    def apply_part(start_row):
        nodal_field = lax.dynamic_slice(first_pad, (zero_index, start_row, zero_index, zero_index), (3, CX + 2, NY + 2, NZ + 2))
        elem_stiff = lax.dynamic_slice(stiff_pad, (start_row, zero_index, zero_index), (CX + 1, NY + 1, NZ + 1))
        return forces(elem_stiff * stiffen(strains(nodal_field)))
    applied = join_slabs(lax.map(apply_part, starts))
    second_sweep = first_sweep + relax_weight * free_nodes * (load_field - applied) / diagonal
    second_pad = padded(second_sweep)

    def sens_part(start_row):
        unit_stress, unit_mises, mises_square, elem_stiff, elem_stress = element_part(start_row)
        unit_stress = unit_stress[:, 1:, 1:, 1:]
        unit_mises = unit_mises[1:, 1:, 1:]
        mises_square = mises_square[1:, 1:, 1:]
        elem_stress = elem_stress[1:, 1:, 1:]
        weight = factor * mises_square ** 3
        adjoint_block = lax.dynamic_slice(second_pad, (zero_index, start_row + 1, one_index, one_index), (3, CX + 1, NY + 1, NZ + 1))
        strain_adj = strains(adjoint_block)
        slope_t = lax.dynamic_slice(stress_slope, (start_row, zero_index, zero_index), (CX, NY, NZ))
        slope_k = lax.dynamic_slice(stiff_slope, (start_row, zero_index, zero_index), (CX, NY, NZ))
        return weight * elem_stress * unit_mises * slope_t - slope_k * lax.optimization_barrier(jnp.sum(strain_adj * unit_stress, axis=0))
    sensitivity = join_slabs(lax.map(sens_part, starts))
    return (second_sweep, sensitivity)
```

```python
import functools
import itertools

import jax
import jax.numpy as jnp
from jax import lax
from jax.experimental import pallas as pl
from jax.experimental.pallas import tpu as pltpu
from jax.sharding import PartitionSpec as P

LAM = 0.577
MU = 0.385
DIAG = (0.577 + 4.0 * 0.385) / 16.0
RELAX = 0.6
SHIFT = 1e-06
BOOST = 2.0**18
MESH = pl.DeviceIdType.MESH
F32 = jnp.float32
ROWS = 48
SIDES = [d for d in itertools.product((-1, 0, 1), repeat=2) if d != (0, 0)]
TILES = [d for d in itertools.product((-1, 0, 1), repeat=3) if d != (0, 0, 0)]
LAST_SIDES = [(-1, 0), (0, -1), (-1, -1)]
LAST_TILES = [(dx, dy, -1) for dx in (0, -1) for dy in (0, -1)]


def span(step):
    return {1: (slice(4, 5), slice(0, 1)), -1: (slice(1, 2), slice(5, 6)), 0: (slice(1, 5), slice(1, 5))}[step]


def rows_of(step):
    return {1: (slice(39, 40), slice(7, 8)), -1: (slice(8, 9), slice(40, 41)), 0: (slice(8, 40), slice(8, 40))}[step]


def kernel(sizes, disp, dens, mat, fix, adj_out, sens_out, *scratch):
    (U, FI, AD, DN, MT, FX, PS, QS, R6, KF, S0, SE, FD, TS, TR, PL, PK, WP, SUM, in_sem,
     f1s, f1r, t1s, t1r, f2s, f2r, t2s, t2r, f3s, f3r, t3s, t3r, ass, asr) = scratch
    nx, ny, nz = sizes
    count = nx * ny * nz * 4 * 32 * 256
    me = (lax.axis_index("gx"), lax.axis_index("gy"), lax.axis_index("gz"))
    lane = lax.broadcasted_iota(jnp.int32, (8, 128), 1)
    first_lane = lane == 0
    last_lane = lane == 127

    def exists(step):
        ok = None
        for i, s, n in zip(me, step, sizes):
            if s:
                one = i < n - 1 if s > 0 else i > 0
                ok = one if ok is None else jnp.logical_and(ok, one)
        return ok

    def at(step):
        return tuple(i + s for i, s in zip(me, step))

    def back(step):
        return tuple(-s for s in step)

    loads = []
    for lt in range(2):
        cols = pl.ds(lt * 128, 128)
        loads.append(pltpu.make_async_copy(disp.at[:, :, :, cols], U.at[0:3, 1:5, lt, 8:40, :], in_sem.at[4 * lt]))
        loads.append(pltpu.make_async_copy(dens.at[:, :, cols], DN.at[:, lt], in_sem.at[4 * lt + 1]))
        loads.append(pltpu.make_async_copy(mat.at[:, :, cols], MT.at[:, lt], in_sem.at[4 * lt + 2]))
        loads.append(pltpu.make_async_copy(fix.at[:, :, cols], FX.at[:, lt], in_sem.at[4 * lt + 3]))
    for c in loads:
        c.start()

    barrier = pltpu.get_barrier_semaphore()

    def greet(device):
        pl.semaphore_signal(barrier, inc=1, device_id=device, device_id_type=MESH)

    for step in TILES:
        pl.when(exists(step))(functools.partial(greet, at(step)))
    rings = []
    for axis, n in enumerate(sizes):
        for k in range(1, n):
            peer = list(me)
            peer[axis] = lax.rem(me[axis] + k, n)
            rings.append((axis, k, tuple(peer)))
            greet(tuple(peer))

    def clear(ref, comps, tile):
        for step, where in (((-1, 0, 0), 0), ((1, 0, 0), 5)):
            def fill(where=where):
                for c in range(comps):
                    for lt in range(2):
                        ref[c, where, lt, 7:41, :] = jnp.full((34, 128), -1.0 if c == 3 else 0.0, F32)
            pl.when(jnp.logical_not(exists(step)))(fill)
        for step, row in (((0, -1, 0), 7), ((0, 1, 0), 40)):
            def fill(row=row):
                for c in range(comps):
                    for x in range(6):
                        for lt in range(2):
                            ref[c, x, lt, row : row + 1, :] = jnp.full((1, 128), -1.0 if c == 3 else 0.0, F32)
            pl.when(jnp.logical_not(exists(step)))(fill)
        for step in TILES:
            def fill(step=step):
                tile[slot(step)] = jnp.where(lane % 32 >= 24, -1.0, 0.0)
            pl.when(jnp.logical_not(exists(back(step))))(fill)

    def slot(step):
        return ((1 - step[2]) * 3 + step[0] + 1) * 3 + step[1] + 1

    clear(U, 4, TR.at[0])
    clear(FI, 3, TR.at[1])
    clear(AD, 3, TR.at[2])
    for c in loads:
        c.wait()

    for x in range(4):
        for lt in range(2):
            m = MT[x, lt]
            U[3, x + 1, lt, 8:40, :] = jnp.where(m == 1, DN[x, lt], jnp.where(m == 2, 1.0, 0.0))

    def pack(ref, comps, high):
        lt, source = (1, 127) if high else (0, 0)
        parts = []
        for g in range(4):
            part = jnp.zeros((8, 128), F32)
            for c in range(comps):
                for x in range(1, 5):
                    to = 32 * g + 8 * c + x
                    v = ref[c, x, lt, 8 + 8 * g : 16 + 8 * g, :]
                    part = jnp.where(lane == to, pltpu.roll(v, (to - source) % 128, 1), part)
            parts.append(part)
        return (parts[0] + parts[1]) + (parts[2] + parts[3])

    def sides(ref, steps, comps_of, send, recv):
        out = []
        for i, (dx, dy) in enumerate(steps):
            (sx, tx), (sr, tr) = span(dx), rows_of(dy)
            comps = slice(0, comps_of(dx, dy))
            out.append(((dx, dy, 0), pltpu.make_async_remote_copy(
                src_ref=ref.at[comps, sx, :, sr, :], dst_ref=ref.at[comps, tx, :, tr, :],
                send_sem=send.at[i], recv_sem=recv.at[i], device_id=at((dx, dy, 0)), device_id_type=MESH)))
        return out

    def tiles(k, steps, send, recv):
        out = []
        for i, step in enumerate(steps):
            out.append((step, pltpu.make_async_remote_copy(
                src_ref=TS.at[k, 1 if step[2] > 0 else 0], dst_ref=TR.at[k, slot(step)],
                send_sem=send.at[i], recv_sem=recv.at[i], device_id=at(step), device_id_type=MESH)))
        return out

    def start(copies):
        for step, c in copies:
            pl.when(exists(step))(c.start)

    def arrive(copies):
        for step, c in copies:
            pl.when(exists(back(step)))(c.wait_recv)

    def left(copies):
        for step, c in copies:
            pl.when(exists(step))(c.wait_send)

    def merge(k, plane, own):
        def tile(dx, dy):
            if plane == 1 and (dx, dy) == (0, 0):
                return own
            return TR[k, (plane * 3 + dx + 1) * 3 + dy + 1]
        for dy in (-1, 0, 1):
            low, mid, high = tile(1, dy), tile(0, dy), tile(-1, dy)
            full = jnp.where(lane % 8 == 0, pltpu.roll(low, 124, 1), jnp.where(lane % 8 == 5, pltpu.roll(high, 4, 1), mid))
            if dy == 0:
                for g in range(4):
                    PL[plane, 8 + 8 * g : 16 + 8 * g, :] = pltpu.roll(full, (128 - 32 * g) % 128, 1) if g else full
            elif dy == 1:
                PL[plane, 0:8, :] = pltpu.roll(full, 32, 1)
            else:
                PL[plane, 40:48, :] = full

    def sweep_z(ref, x_from):
        def body(g, carry):
            rows = pl.ds(7 + 8 * g, 8)
            edge = PL[2, rows, :]
            for c in range(3):
                for x in range(x_from, 6):
                    t0, t1 = ref[c, x, 0, rows, :], ref[c, x, 1, rows, :]
                    r0, r1 = pltpu.roll(t0, 127, 1), pltpu.roll(t1, 127, 1)
                    s0 = jnp.where(last_lane, r1, r0)
                    s1 = jnp.where(last_lane, pltpu.roll(edge, (127 - 8 * c - x) % 128, 1), r1)
                    PS[c, x, 0, rows, :] = s0 + t0
                    PS[c, x, 1, rows, :] = s1 + t1
                    QS[c, x, 0, rows, :] = s0 - t0
                    QS[c, x, 1, rows, :] = s1 - t1
            return carry
        lax.fori_loop(0, 5, body, 0)

    def gradients(low, high):
        return [[high[c][0] - low[c][0] for c in range(3)], [high[c][1] + low[c][1] for c in range(3)],
                [high[c][2] + low[c][2] for c in range(3)]]

    def strain6(g):
        gx, gy, gz = g
        return gx[0], gy[1], gz[2], gy[0] + gx[1], gz[1] + gy[2], gx[2] + gz[0]

    def y_sums(x, lt, base):
        out = []
        for c in range(3):
            p0, p1 = PS[c, x, lt, pl.ds(base, 8), :], PS[c, x, lt, pl.ds(base + 1, 8), :]
            q0, q1 = QS[c, x, lt, pl.ds(base, 8), :], QS[c, x, lt, pl.ds(base + 1, 8), :]
            out.append((p0 + p1, p1 - p0, q0 + q1))
        return out

    def packed_strain(k):
        lo, hi = PL[0], PL[1]
        PK[0] = lo + hi
        PK[1] = hi - lo
        p0, p1, q0, q1 = PK[0, 0:40], PK[0, 1:41], PK[1, 0:40], PK[1, 1:41]
        a, b, c = p0 + p1, p1 - p0, q0 + q1
        g = [pltpu.roll(a, 127, 1) - a, pltpu.roll(b, 127, 1) + b, pltpu.roll(c, 127, 1) + c]
        return strain6([[t] + [pltpu.roll(t, 128 - 8 * i, 1) for i in (1, 2)] for t in g])

    def load_terms(e, d):
        a, b, c = e[0] - e[1], e[1] - e[2], e[2] - e[0]
        q = (MU * MU / 16.0) * (2.0 * (a * a + b * b + c * c) + 3.0 * (e[3] * e[3] + e[4] * e[4] + e[5] * e[5]))
        vm = d * q
        w = vm * vm * vm
        t = (-MU * MU / 8.0 * BOOST) * (w * d)
        ts = 1.5 * t
        return q, vm, w, (t * (a - c), t * (b - a), t * (c - b), ts * e[3], ts * e[4], ts * e[5])

    def stiff_terms(e, kf):
        k = kf * (-2.0 * MU / 16.0)
        tr = (kf * (-LAM / 16.0)) * (e[0] + e[1] + e[2])
        ks = kf * (-MU / 16.0)
        return tr + k * e[0], tr + k * e[1], tr + k * e[2], ks * e[3], ks * e[4], ks * e[5]

    S_Y, D_Y = (0, 3, 5, 4, 2), (3, 1, 4)

    def x_parts(low, high):
        (sl, dl), (sh, dh) = low, high
        return [((sh[i] - sl[i]) + (dh[j] + dl[j]), sh[k] + sl[k]) for i, j, k in ((0, 3, 5), (3, 1, 4), (5, 4, 2))]

    def packed_forces(r):
        for i in range(6):
            PK[i, 0:40] = r[i]
        s = {i: PK[i, 7:39] + PK[i, 8:40] for i in S_Y}
        d = {i: PK[i, 8:40] - PK[i, 7:39] for i in D_Y}
        high = ({i: pltpu.roll(v, 127, 1) for i, v in s.items()}, {i: pltpu.roll(v, 127, 1) for i, v in d.items()})
        for c, (u, w) in enumerate(x_parts((s, d), high)):
            WP[c] = u - w

    def from_low(w0, w1, packed, x):
        r0, r1 = pltpu.roll(w0, 1, 1), pltpu.roll(w1, 1, 1)
        edge = pltpu.roll(packed, (128 - x) % 128, 1) if x else packed
        return jnp.where(first_lane, edge, r0), jnp.where(first_lane, r0, r1)

    def forces(finish):
        def body(g, carry):
            base = pl.multiple_of(8 + 8 * g, 8)
            own = pl.ds(pl.multiple_of(8 * g, 8), 8)
            packed = [WP[c, own, :] for c in range(3)]

            def sums(x):
                out = []
                for lt in range(2):
                    r1 = [R6[i, x, lt, pl.ds(base, 8), :] for i in range(6)]
                    r0 = [R6[i, x, lt, pl.ds(base - 1, 8), :] for i in range(6)]
                    out.append(({i: r0[i] + r1[i] for i in S_Y}, {i: r1[i] - r0[i] for i in D_Y}))
                return out

            low = sums(0)
            for x in range(4):
                high = sums(x + 1)
                p0, p1 = x_parts(low[0], high[0]), x_parts(low[1], high[1])
                for c in range(3):
                    (u0, c0), (u1, c1) = p0[c], p1[c]
                    s0, s1 = from_low(u0 - c0, u1 - c1, packed[c], x)
                    finish(c, x, 0, base, own, u0 + c0 + s0)
                    finish(c, x, 1, base, own, u1 + c1 + s1)
                low = high
            return carry
        lax.fori_loop(0, 4, body, 0)

    own_tile = pack(U, 4, False)
    TS[0, 0] = own_tile
    TS[0, 1] = pack(U, 4, True)

    block = 1
    for i, n in zip(me, sizes):
        block = block * (1 + (i > 0).astype(jnp.int32) + (i < n - 1).astype(jnp.int32))
    pl.semaphore_wait(barrier, block - 1 + len(rings))

    t1 = tiles(0, TILES, t1s, t1r)
    f1 = sides(U, SIDES, lambda dx, dy: 4 if dx >= 0 and dy >= 0 else 3, f1s, f1r)
    start(t1)
    start(f1)
    arrive(t1)
    arrive(f1)

    for plane in range(3):
        merge(0, plane, own_tile)
    d = pltpu.roll(PL[0, 0:40, :], 104, 1)
    kp = jnp.where(d < 0.0, 0.0, 0.001 + d * d * d)
    e = packed_strain(0)
    r = load_terms(e, jnp.maximum(d, 0.0))[3]
    packed_forces(r)
    PK[6, 0:40] = kp
    ky = PK[6, 7:39] + PK[6, 8:40]
    WP[3] = ky + pltpu.roll(ky, 127, 1)
    sweep_z(U, 0)

    def power_body(g, total):
        base = pl.multiple_of(8 * g, 8)
        rows = pl.ds(base, 8)
        own = pl.ds(pl.multiple_of(jnp.maximum(8 * g - 8, 0), 8), 8)
        inside = (g > 0).astype(F32)
        for lt in range(2):
            low = y_sums(0, lt, base)
            for x in range(5):
                high = y_sums(x + 1, lt, base)
                e = strain6(gradients(low, high))
                low = high
                d = U[3, x, lt, rows, :]
                KF[x, lt, rows, :] = jnp.where(d < 0.0, 0.0, 0.001 + d * d * d)
                q, vm, w, r = load_terms(e, jnp.maximum(d, 0.0))
                for i in range(6):
                    R6[i, x, lt, rows, :] = r[i]
                if x > 0:
                    v2 = vm * vm
                    total = total + jnp.where(inside > 0.0, v2 * v2, 0.0)
                    tr = (LAM / 16.0) * (e[0] + e[1] + e[2])
                    for i in range(6):
                        S0[i, x - 1, lt, own, :] = tr + (MU / 8.0) * e[i] if i < 3 else (MU / 16.0) * e[i]
                    design = MT[x - 1, lt, own, :] == 1
                    SE[x - 1, lt, own, :] = jnp.where(design, (0.5 * BOOST) * (w * q), 0.0)
        return total

    total = lax.fori_loop(0, 5, power_body, jnp.zeros((8, 128), F32))

    order = (2, 1, 0)

    def ring(stage):
        axis, out = order[stage], []
        for i, (a, k, peer) in enumerate(rings):
            if a == axis:
                out.append(pltpu.make_async_remote_copy(
                    src_ref=SUM.at[stage, me[axis]], dst_ref=SUM.at[stage, me[axis]],
                    send_sem=ass.at[i], recv_sem=asr.at[i], device_id=peer, device_id_type=MESH))
        return out

    def send_sum(stage, value):
        SUM[stage, me[order[stage]]] = value
        for c in ring(stage):
            c.start()

    def take_sum(stage):
        for c in ring(stage):
            c.wait_recv()
        value = SUM[stage, 0]
        for i in range(1, sizes[order[stage]]):
            value = value + SUM[stage, i]
        return value

    send_sum(0, total)

    def diag_body(g, carry):
        base = pl.multiple_of(8 + 8 * g, 8)
        own = pl.ds(pl.multiple_of(8 * g, 8), 8)
        packed = WP[3, own, :]

        def sums(x):
            return [KF[x, lt, pl.ds(base, 8), :] + KF[x, lt, pl.ds(base - 1, 8), :] for lt in range(2)]

        low = sums(0)
        for x in range(4):
            high = sums(x + 1)
            k0, k1 = low[0] + high[0], low[1] + high[1]
            s0, s1 = from_low(k0, k1, packed, x)
            for lt, k in ((0, k0 + s0), (1, k1 + s1)):
                fixed = FX[x, lt, own, :].astype(F32)
                FD[x, lt, own, :] = (1.0 - fixed) / (DIAG * k + fixed)
            low = high
        return carry

    lax.fori_loop(0, 4, diag_body, 0)

    def first_out(c, x, lt, base, own, value):
        FI[c, x + 1, lt, pl.ds(base, 8), :] = value * FD[x, lt, own, :]

    forces(first_out)

    own_tile = pack(FI, 3, False)
    TS[1, 0] = own_tile
    TS[1, 1] = pack(FI, 3, True)
    t2 = tiles(1, TILES, t2s, t2r)
    f2 = sides(FI, SIDES, lambda dx, dy: 3, f2s, f2r)
    start(t2)
    start(f2)
    send_sum(1, take_sum(0))
    arrive(t2)
    arrive(f2)
    for plane in range(3):
        merge(1, plane, own_tile)
    packed_forces_in = packed_strain(1)
    packed_forces(stiff_terms(packed_forces_in, kp))
    sweep_z(FI, 0)

    def stiff_body(g, carry):
        base = pl.multiple_of(8 * g, 8)
        rows = pl.ds(base, 8)
        for lt in range(2):
            low = y_sums(0, lt, base)
            for x in range(5):
                high = y_sums(x + 1, lt, base)
                r = stiff_terms(strain6(gradients(low, high)), KF[x, lt, rows, :])
                low = high
                for i in range(6):
                    R6[i, x, lt, rows, :] = r[i]
        return carry

    lax.fori_loop(0, 5, stiff_body, 0)
    send_sum(2, take_sum(1))

    def adjoint_out(c, x, lt, base, own, value):
        AD[c, x + 1, lt, pl.ds(base, 8), :] = (1.0 + RELAX) * FI[c, x + 1, lt, pl.ds(base, 8), :] - RELAX * FD[x, lt, own, :] * value

    forces(adjoint_out)

    TS[2, 0] = pack(AD, 3, False)
    t3 = tiles(2, LAST_TILES, t3s, t3r)
    f3 = sides(AD, LAST_SIDES, lambda dx, dy: 3, f3s, f3r)
    start(t3)
    start(f3)
    arrive(t3)
    arrive(f3)
    merge(2, 2, None)
    sweep_z(AD, 1)

    total = jnp.sum(take_sum(2)) * (1.0 / count) + SHIFT
    total = jnp.full((8, 128), total, F32)
    scale = jnp.sqrt(jnp.sqrt(jnp.sqrt(total))) / total * (1.0 / BOOST)

    def last_body(g, carry):
        base = pl.multiple_of(8 + 8 * g, 8)
        rows = pl.ds(base, 8)
        own = pl.ds(pl.multiple_of(8 * g, 8), 8)
        for lt in range(2):
            cols = slice(128 * lt, 128 * lt + 128)
            low = y_sums(1, lt, base)
            for x in range(4):
                high = y_sums(x + 2, lt, base)
                e = strain6(gradients(low, high))
                low = high
                dot = e[0] * S0[0, x, lt, own, :]
                for i in range(1, 6):
                    dot = dot + e[i] * S0[i, x, lt, own, :]
                d = U[3, x + 1, lt, rows, :]
                slope = jnp.where(MT[x, lt, own, :] == 1, 3.0 * (d * d), 0.0)
                sens_out[x, own, cols] = scale * (SE[x, lt, own, :] - slope * dot)
                for c in range(3):
                    adj_out[c, x, own, cols] = scale * AD[c, x + 1, lt, rows, :]
        return carry

    lax.fori_loop(0, 4, last_body, 0)
    for copies in (t1, f1, t2, f2, t3, f3):
        left(copies)
    for stage in range(3):
        for c in ring(stage):
            c.wait_send()


def solution(mesh):
    sizes = tuple(mesh.shape[a] for a in ("gx", "gy", "gz"))
    peers = sum(sizes) - 3

    def per_device(displacement, density, material, fixed_mask):
        dma = pltpu.SemaphoreType.DMA
        return pl.pallas_call(
            functools.partial(kernel, sizes),
            out_shape=(jax.ShapeDtypeStruct((3, 4, 32, 256), F32), jax.ShapeDtypeStruct((4, 32, 256), F32)),
            in_specs=[pl.BlockSpec(memory_space=pl.ANY)] * 4,
            out_specs=[pl.BlockSpec(memory_space=pltpu.VMEM)] * 2,
            scratch_shapes=[
                pltpu.VMEM((4, 6, 2, ROWS, 128), F32),
                pltpu.VMEM((3, 6, 2, ROWS, 128), F32),
                pltpu.VMEM((3, 6, 2, ROWS, 128), F32),
                pltpu.VMEM((4, 2, 32, 128), F32),
                pltpu.VMEM((4, 2, 32, 128), jnp.int32),
                pltpu.VMEM((4, 2, 32, 128), jnp.int32),
                pltpu.VMEM((3, 6, 2, ROWS, 128), F32),
                pltpu.VMEM((3, 6, 2, ROWS, 128), F32),
                pltpu.VMEM((6, 5, 2, ROWS, 128), F32),
                pltpu.VMEM((5, 2, ROWS, 128), F32),
                pltpu.VMEM((6, 4, 2, 32, 128), F32),
                pltpu.VMEM((4, 2, 32, 128), F32),
                pltpu.VMEM((4, 2, 32, 128), F32),
                pltpu.VMEM((3, 2, 8, 128), F32),
                pltpu.VMEM((3, 27, 8, 128), F32),
                pltpu.VMEM((3, ROWS, 128), F32),
                pltpu.VMEM((7, ROWS, 128), F32),
                pltpu.VMEM((4, 32, 128), F32),
                pltpu.VMEM((3, 8, 8, 128), F32),
                dma((8,)),
                dma((8,)), dma((8,)), dma((26,)), dma((26,)),
                dma((8,)), dma((8,)), dma((26,)), dma((26,)),
                dma((3,)), dma((3,)), dma((4,)), dma((4,)),
                dma((peers,)), dma((peers,)),
            ],
            compiler_params=pltpu.CompilerParams(collective_id=0, has_side_effects=True),
        )(displacement, density, material, fixed_mask)

    placed = (P(None, "gx", "gy", "gz"), P("gx", "gy", "gz"), P("gx", "gy", "gz"), P("gx", "gy", "gz"))
    return jax.shard_map(per_device, mesh=mesh, in_specs=placed, out_specs=(placed[0], placed[1]), check_vma=False)
```

```python
import functools
import itertools

import jax
import jax.numpy as jnp
from jax import lax
from jax.experimental import pallas as pl
from jax.experimental.pallas import tpu as pltpu
from jax.sharding import PartitionSpec as P

LAM = 0.577
MU = 0.385
DIAG = (0.577 + 4.0 * 0.385) / 16.0
RELAX = 0.6
SHIFT = 1e-06
BOOST = 2.0**18
MESH = pl.DeviceIdType.MESH
F32 = jnp.float32
ROWS = 48
NEAR = [d for d in itertools.product((-1, 0, 1), repeat=3) if d != (0, 0, 0)]
SIDES = [d for d in itertools.product((-1, 0, 1), repeat=2) if d != (0, 0)]
TILES = [d for d in NEAR if d[0] == 0]
LINES = [d for d in NEAR if d[0] != 0]
LAST_SIDES = [(-1, 0), (-1, -1), (0, -1)]
LAST_TILES = [(0, 0, -1), (0, -1, -1)]
LAST_LINES = [(-1, 0, -1), (-1, -1, -1)]


def span(step):
    return {1: (slice(4, 5), slice(0, 1)), -1: (slice(1, 2), slice(5, 6)), 0: (slice(1, 5), slice(1, 5))}[step]


def rows_of(step):
    return {1: (slice(39, 40), slice(7, 8)), -1: (slice(8, 9), slice(40, 41)), 0: (slice(8, 40), slice(8, 40))}[step]


def kernel(sizes, disp, dens, mat, fix, adj_out, sens_out, sum_out, *scratch):
    (U, FI, AD, DN, MT, FX, PS, QS, R6, KF, S0, SE, FD, TS, LS, TR, LR, PL, PK, WP, SUM, in_sem,
     f1s, f1r, t1s, t1r, l1s, l1r, f2s, f2r, t2s, t2r, l2s, l2r, f3s, f3r, t3s, t3r, l3s, l3r, ass, asr) = scratch
    nx, ny, nz = sizes
    me = (lax.axis_index("gx"), lax.axis_index("gy"), lax.axis_index("gz"))
    lane = lax.broadcasted_iota(jnp.int32, (8, 128), 1)
    sub = lax.broadcasted_iota(jnp.int32, (8, 128), 0)
    first_lane = lane == 0
    last_lane = lane == 127

    def exists(step):
        ok = None
        for i, s, n in zip(me, step, sizes):
            if s:
                one = i < n - 1 if s > 0 else i > 0
                ok = one if ok is None else jnp.logical_and(ok, one)
        return ok

    def at(step):
        return tuple(i + s for i, s in zip(me, step))

    def back(step):
        return tuple(-s for s in step)

    barrier = pltpu.get_barrier_semaphore()

    def greet(device):
        pl.semaphore_signal(barrier, inc=1, device_id=device, device_id_type=MESH)

    rings = []
    for axis, n in enumerate(sizes):
        for k in range(1, n):
            peer = list(me)
            peer[axis] = lax.rem(me[axis] + k, n)
            rings.append((axis, k, tuple(peer)))
            greet(tuple(peer))
    for step in NEAR:
        pl.when(exists(step))(functools.partial(greet, at(step)))

    loads = []
    for lt in range(2):
        cols = pl.ds(lt * 128, 128)
        loads.append(pltpu.make_async_copy(disp.at[:, :, :, cols], U.at[0:3, 1:5, lt, 8:40, :], in_sem.at[4 * lt]))
        loads.append(pltpu.make_async_copy(dens.at[:, :, cols], DN.at[:, lt], in_sem.at[4 * lt + 1]))
        loads.append(pltpu.make_async_copy(mat.at[:, :, cols], MT.at[:, lt], in_sem.at[4 * lt + 2]))
        loads.append(pltpu.make_async_copy(fix.at[:, :, cols], FX.at[:, lt], in_sem.at[4 * lt + 3]))
    for c in loads:
        c.start()

    def plane_of(step):
        return 1 - step[2]

    def clear(k, ref, comps):
        for step, where in (((-1, 0, 0), 0), ((1, 0, 0), 5)):
            def fill(where=where):
                for c in range(comps):
                    for lt in range(2):
                        ref[c, where, lt, 7:41, :] = jnp.full((34, 128), -1.0 if c == 3 else 0.0, F32)
            pl.when(jnp.logical_not(exists(step)))(fill)
        for step, row in (((0, -1, 0), 7), ((0, 1, 0), 40)):
            def fill(row=row):
                for c in range(comps):
                    for x in range(6):
                        for lt in range(2):
                            ref[c, x, lt, row : row + 1, :] = jnp.full((1, 128), -1.0 if c == 3 else 0.0, F32)
            pl.when(jnp.logical_not(exists(step)))(fill)
        outside = jnp.where(lane % 4 == 3, -1.0, 0.0)
        for step in TILES:
            def fill(step=step):
                TR[k, plane_of(step), step[1] + 1] = outside
            pl.when(jnp.logical_not(exists(back(step))))(fill)
        for step in LINES:
            def fill(step=step):
                LR[k, plane_of(step), (step[0] + 1) // 2, step[1] + 1] = outside[0:1]
            pl.when(jnp.logical_not(exists(back(step))))(fill)

    clear(0, U, 4)
    clear(1, FI, 3)
    clear(2, AD, 3)
    for c in loads:
        c.wait()

    for x in range(4):
        for lt in range(2):
            m = MT[x, lt]
            U[3, x + 1, lt, 8:40, :] = jnp.where(m == 1, DN[x, lt], jnp.where(m == 2, 1.0, 0.0))

    def pack(ref, comps, high, xs):
        lt, source = (1, 127) if high else (0, 0)
        parts = []
        for g in range(4):
            part = jnp.zeros((8, 128), F32)
            for c in range(comps):
                for x in xs:
                    to = 32 * g + 4 * x + c
                    v = ref[c, x, lt, 8 + 8 * g : 16 + 8 * g, :]
                    part = jnp.where(lane == to, pltpu.roll(v, (to - source) % 128, 1), part)
            parts.append(part)
        return (parts[0] + parts[1]) + (parts[2] + parts[3])

    def line(tile, x):
        out = jnp.zeros((8, 128), F32)
        mine = (lane % 32) // 4 == 7 - sub
        for i in range(8):
            out = jnp.where(jnp.logical_and(mine, sub == i), pltpu.roll(tile, (28 - 4 * i - 4 * x) % 128, 1), out)
        return jnp.sum(out, axis=0, keepdims=True)

    def spread(row, x):
        moved = pltpu.roll(jnp.broadcast_to(row, (8, 128)), 0, 1, stride=4, stride_axis=0)
        return pltpu.roll(moved, (100 + 4 * x) % 128, 1)

    def remote(src, dst, send, recv, step):
        return (step, pltpu.make_async_remote_copy(
            src_ref=src, dst_ref=dst, send_sem=send, recv_sem=recv, device_id=at(step), device_id_type=MESH))

    def sides(ref, steps, comps_of, send, recv):
        out = []
        for i, (dx, dy) in enumerate(steps):
            (sx, tx), (sr, tr) = span(dx), rows_of(dy)
            comps = slice(0, comps_of(dx, dy))
            out.append(remote(ref.at[comps, sx, :, sr, :], ref.at[comps, tx, :, tr, :], send.at[i], recv.at[i], (dx, dy, 0)))
        return out

    def tiles(k, steps, send, recv):
        return [remote(TS.at[k, 1 if step[2] > 0 else 0], TR.at[k, plane_of(step), step[1] + 1], send.at[i], recv.at[i], step)
                for i, step in enumerate(steps)]

    def lines(k, steps, send, recv):
        return [remote(LS.at[k, 1 if step[2] > 0 else 0, (step[0] + 1) // 2],
                       LR.at[k, plane_of(step), (step[0] + 1) // 2, step[1] + 1], send.at[i], recv.at[i], step)
                for i, step in enumerate(steps)]

    def along(copies):
        return [c for c in copies if c[0][0] == 0], [c for c in copies if c[0][0] != 0]

    def start(copies):
        for step, c in copies:
            pl.when(exists(step))(c.start)

    def arrive(copies):
        for step, c in copies:
            pl.when(exists(back(step)))(c.wait_recv)

    def left(copies):
        for step, c in copies:
            pl.when(exists(step))(c.wait_send)

    def merge(k, plane, with_x):
        for dy in (-1, 0, 1):
            full = TS[k, 0] if plane == 1 and dy == 0 else TR[k, plane, dy + 1]
            if with_x:
                full = jnp.where(lane % 32 < 4, spread(LR[k, plane, 1, dy + 1], 0), full)
                full = jnp.where(lane % 32 >= 20, spread(LR[k, plane, 0, dy + 1], 5), full)
            if dy == 0:
                for g in range(4):
                    PL[plane, 8 + 8 * g : 16 + 8 * g, :] = pltpu.roll(full, (128 - 32 * g) % 128, 1) if g else full
            elif dy == 1:
                PL[plane, 0:8, :] = pltpu.roll(full, 32, 1)
            else:
                PL[plane, 40:48, :] = full

    def sweep_z(ref, xs):
        def body(g, carry):
            rows = pl.ds(7 + 8 * g, 8)
            edge = PL[2, rows, :]
            for c in range(3):
                for x in xs:
                    t0, t1 = ref[c, x, 0, rows, :], ref[c, x, 1, rows, :]
                    r0, r1 = pltpu.roll(t0, 127, 1), pltpu.roll(t1, 127, 1)
                    s0 = jnp.where(last_lane, r1, r0)
                    s1 = jnp.where(last_lane, pltpu.roll(edge, 127 - 4 * x - c, 1), r1)
                    PS[c, x, 0, rows, :] = s0 + t0
                    PS[c, x, 1, rows, :] = s1 + t1
                    QS[c, x, 0, rows, :] = s0 - t0
                    QS[c, x, 1, rows, :] = s1 - t1
            return carry
        lax.fori_loop(0, 5, body, 0)

    def gradients(low, high):
        return [[high[c][0] - low[c][0] for c in range(3)], [high[c][1] + low[c][1] for c in range(3)],
                [high[c][2] + low[c][2] for c in range(3)]]

    def strain6(g):
        gx, gy, gz = g
        return gx[0], gy[1], gz[2], gy[0] + gx[1], gz[1] + gy[2], gx[2] + gz[0]

    def y_sums(x, lt, base):
        out = []
        for c in range(3):
            p0, p1 = PS[c, x, lt, pl.ds(base, 8), :], PS[c, x, lt, pl.ds(base + 1, 8), :]
            q0, q1 = QS[c, x, lt, pl.ds(base, 8), :], QS[c, x, lt, pl.ds(base + 1, 8), :]
            out.append((p0 + p1, p1 - p0, q0 + q1))
        return out

    def packed_strain():
        lo, hi = PL[0], PL[1]
        PK[0] = lo + hi
        PK[1] = hi - lo
        p0, p1, q0, q1 = PK[0, 0:40], PK[0, 1:41], PK[1, 0:40], PK[1, 1:41]
        a, b, c = p0 + p1, p1 - p0, q0 + q1
        g = [pltpu.roll(a, 124, 1) - a, pltpu.roll(b, 124, 1) + b, pltpu.roll(c, 124, 1) + c]
        return strain6([[t] + [pltpu.roll(t, 128 - i, 1) for i in (1, 2)] for t in g])

    def stiffness(d):
        return jnp.where(d < 0.0, 0.0, 0.001 + d * d * d)

    def load_terms(e, d):
        a, b, c = e[0] - e[1], e[1] - e[2], e[2] - e[0]
        q = (MU * MU / 16.0) * (2.0 * (a * a + b * b + c * c) + 3.0 * (e[3] * e[3] + e[4] * e[4] + e[5] * e[5]))
        vm = d * q
        w = vm * vm * vm
        t = (-MU * MU / 8.0 * BOOST) * (w * d)
        ts = 1.5 * t
        return q, vm, w, (t * (a - c), t * (b - a), t * (c - b), ts * e[3], ts * e[4], ts * e[5])

    def stiff_terms(e, kf):
        k = kf * (-2.0 * MU / 16.0)
        tr = (kf * (-LAM / 16.0)) * (e[0] + e[1] + e[2])
        ks = kf * (-MU / 16.0)
        return tr + k * e[0], tr + k * e[1], tr + k * e[2], ks * e[3], ks * e[4], ks * e[5]

    S_Y, D_Y = (0, 3, 5, 4, 2), (3, 1, 4)

    def x_parts(low, high):
        (sl, dl), (sh, dh) = low, high
        return [((sh[i] - sl[i]) + (dh[j] + dl[j]), sh[k] + sl[k]) for i, j, k in ((0, 3, 5), (3, 1, 4), (5, 4, 2))]

    def packed_forces(r):
        for i in range(6):
            PK[i, 0:40] = r[i]
        s = {i: PK[i, 7:39] + PK[i, 8:40] for i in S_Y}
        d = {i: PK[i, 8:40] - PK[i, 7:39] for i in D_Y}
        high = ({i: pltpu.roll(v, 124, 1) for i, v in s.items()}, {i: pltpu.roll(v, 124, 1) for i, v in d.items()})
        for c, (u, w) in enumerate(x_parts((s, d), high)):
            WP[c] = u - w

    def from_low(w0, w1, packed, x):
        r0, r1 = pltpu.roll(w0, 1, 1), pltpu.roll(w1, 1, 1)
        edge = pltpu.roll(packed, 128 - 4 * x, 1) if x else packed
        return jnp.where(first_lane, edge, r0), jnp.where(first_lane, r0, r1)

    def forces(xs, finish):
        def body(g, carry):
            base = pl.multiple_of(8 + 8 * g, 8)
            own = pl.ds(pl.multiple_of(8 * g, 8), 8)
            packed = [WP[c, own, :] for c in range(3)]

            def sums(x):
                out = []
                for lt in range(2):
                    r1 = [R6[i, x, lt, pl.ds(base, 8), :] for i in range(6)]
                    r0 = [R6[i, x, lt, pl.ds(base - 1, 8), :] for i in range(6)]
                    out.append(({i: r0[i] + r1[i] for i in S_Y}, {i: r1[i] - r0[i] for i in D_Y}))
                return out

            low = sums(xs[0])
            for x in xs:
                high = sums(x + 1)
                p0, p1 = x_parts(low[0], high[0]), x_parts(low[1], high[1])
                for c in range(3):
                    (u0, c0), (u1, c1) = p0[c], p1[c]
                    s0, s1 = from_low(u0 - c0, u1 - c1, packed[c], x)
                    finish(c, x, 0, base, own, u0 + c0 + s0)
                    finish(c, x, 1, base, own, u1 + c1 + s1)
                low = high
            return carry
        lax.fori_loop(0, 4, body, 0)

    def send_tiles(k, ref, comps, copies):
        TS[k, 0] = pack(ref, comps, False, range(1, 5))
        TS[k, 1] = pack(ref, comps, True, range(1, 5))
        start(copies)

    def put_lines(k, low, high):
        for z, t in enumerate((low, high)):
            LS[k, z, 0] = line(t, 1)
            LS[k, z, 1] = line(t, 4)

    TS[0, 0] = pack(U, 4, False, range(1, 5))
    TS[0, 1] = pack(U, 4, True, range(1, 5))
    put_lines(0, TS[0, 0], TS[0, 1])

    t1 = tiles(0, TILES, t1s, t1r)
    l1 = lines(0, LINES, l1s, l1r)
    f1, x1 = along(sides(U, SIDES, lambda dx, dy: 4 if dx >= 0 and dy >= 0 else 3, f1s, f1r))
    t2 = tiles(1, TILES, t2s, t2r)
    l2 = lines(1, LINES, l2s, l2r)
    f2, x2 = along(sides(FI, SIDES, lambda dx, dy: 3, f2s, f2r))
    t3 = tiles(2, LAST_TILES, t3s, t3r)
    l3 = lines(2, LAST_LINES, l3s, l3r)
    f3, x3 = along(sides(AD, LAST_SIDES, lambda dx, dy: 3, f3s, f3r))

    block = 1
    for i, n in zip(me, sizes):
        block = block * (1 + (i > 0).astype(jnp.int32) + (i < n - 1).astype(jnp.int32))
    pl.semaphore_wait(barrier, block - 1 + len(rings))

    start(l1)
    start(x1)
    start(t1)
    start(f1)

    def power(xs, total):
        def body(g, total):
            base = pl.multiple_of(8 * g, 8)
            rows = pl.ds(base, 8)
            own = pl.ds(pl.multiple_of(jnp.maximum(8 * g - 8, 0), 8), 8)
            inside = jnp.full((8, 128), g, jnp.int32) > 0
            for lt in range(2):
                low = y_sums(xs[0], lt, base)
                for x in xs:
                    high = y_sums(x + 1, lt, base)
                    e = strain6(gradients(low, high))
                    low = high
                    q, vm, w, r = load_terms(e, jnp.maximum(U[3, x, lt, rows, :], 0.0))
                    for i in range(6):
                        R6[i, x, lt, rows, :] = r[i]
                    if x > 0:
                        v2 = vm * vm
                        total = total + jnp.where(inside, v2 * v2, 0.0)
                        tr = (LAM / 16.0) * (e[0] + e[1] + e[2])
                        for i in range(6):
                            S0[i, x - 1, lt, own, :] = tr + (MU / 8.0) * e[i] if i < 3 else (MU / 16.0) * e[i]
                        SE[x - 1, lt, own, :] = jnp.where(MT[x - 1, lt, own, :] == 1, (0.5 * BOOST) * (w * q), 0.0)
            return total
        return lax.fori_loop(0, 5, body, total)

    def fill_stiffness(xs):
        for x in xs:
            for lt in range(2):
                KF[x, lt, 0:40, :] = stiffness(U[3, x, lt, 0:40, :])

    def packed_load():
        d = pltpu.roll(PL[0, 0:40, :], 125, 1)
        kp = stiffness(d)
        packed_forces(load_terms(packed_strain(), jnp.maximum(d, 0.0))[3])
        PK[6, 0:40] = kp
        ky = PK[6, 7:39] + PK[6, 8:40]
        WP[3] = ky + pltpu.roll(ky, 124, 1)

    def diagonal(xs):
        def body(g, carry):
            base = pl.multiple_of(8 + 8 * g, 8)
            own = pl.ds(pl.multiple_of(8 * g, 8), 8)
            packed = WP[3, own, :]

            def sums(x):
                return [KF[x, lt, pl.ds(base, 8), :] + KF[x, lt, pl.ds(base - 1, 8), :] for lt in range(2)]

            low = sums(xs[0])
            for x in xs:
                high = sums(x + 1)
                k0, k1 = low[0] + high[0], low[1] + high[1]
                s0, s1 = from_low(k0, k1, packed, x)
                for lt, k in ((0, k0 + s0), (1, k1 + s1)):
                    fixed = FX[x, lt, own, :].astype(F32)
                    FD[x, lt, own, :] = (1.0 - fixed) / (DIAG * k + fixed)
                low = high
            return carry
        lax.fori_loop(0, 4, body, 0)

    def first_out(c, x, lt, base, own, value):
        FI[c, x + 1, lt, pl.ds(base, 8), :] = value * FD[x, lt, own, :]

    arrive(t1)
    arrive(f1)
    for plane in range(3):
        merge(0, plane, False)
    packed_load()
    sweep_z(U, range(1, 5))
    total = power((1, 2, 3), jnp.zeros((8, 128), F32))
    fill_stiffness(range(1, 5))
    diagonal((1, 2, 3))
    forces((1, 2), first_out)

    arrive(l1)
    arrive(x1)
    for plane in range(3):
        merge(0, plane, True)
    packed_load()
    sweep_z(U, (0, 5))
    fill_stiffness((0,))
    diagonal((0,))
    power((0,), total)
    total = power((4,), total)
    forces((0,), first_out)
    forces((3,), first_out)
    start(x2)
    TS[1, 0] = pack(FI, 3, False, range(1, 5))
    TS[1, 1] = pack(FI, 3, True, range(1, 5))
    put_lines(1, TS[1, 0], TS[1, 1])
    start(l2)
    start(t2)
    start(f2)

    order = (2, 1, 0)

    def ring(stage):
        axis, out = order[stage], []
        for i, (a, k, peer) in enumerate(rings):
            if a == axis:
                out.append(pltpu.make_async_remote_copy(
                    src_ref=SUM.at[stage, me[axis]], dst_ref=SUM.at[stage, me[axis]],
                    send_sem=ass.at[i], recv_sem=asr.at[i], device_id=peer, device_id_type=MESH))
        return out

    def send_sum(stage, value):
        SUM[stage, me[order[stage]]] = value
        for c in ring(stage):
            c.start()

    def take_sum(stage):
        for c in ring(stage):
            c.wait_recv()
        value = SUM[stage, 0]
        for i in range(1, sizes[order[stage]]):
            value = value + SUM[stage, i]
        return value

    send_sum(0, total)

    def stiff(xs):
        def body(g, carry):
            base = pl.multiple_of(8 * g, 8)
            rows = pl.ds(base, 8)
            for lt in range(2):
                low = y_sums(xs[0], lt, base)
                for x in xs:
                    high = y_sums(x + 1, lt, base)
                    r = stiff_terms(strain6(gradients(low, high)), KF[x, lt, rows, :])
                    low = high
                    for i in range(6):
                        R6[i, x, lt, rows, :] = r[i]
            return carry
        lax.fori_loop(0, 5, body, 0)

    def packed_stiff():
        packed_forces(stiff_terms(packed_strain(), kp_ref[...]))

    def adjoint_out(c, x, lt, base, own, value):
        new = (1.0 + RELAX) * FI[c, x + 1, lt, pl.ds(base, 8), :] - RELAX * FD[x, lt, own, :] * value
        AD[c, x + 1, lt, pl.ds(base, 8), :] = new
        adj_out[c, x, lt, own, :] = new

    kp_ref = PK.at[6, 0:40]
    arrive(t2)
    arrive(f2)
    for plane in range(3):
        merge(1, plane, False)
    packed_stiff()
    sweep_z(FI, range(1, 5))
    stiff((1, 2, 3))
    forces((1, 2), adjoint_out)
    send_sum(1, take_sum(0))
    arrive(l2)
    arrive(x2)
    for plane in range(3):
        merge(1, plane, True)
    packed_stiff()
    sweep_z(FI, (0, 5))
    stiff((0,))
    forces((0,), adjoint_out)
    start(x3)
    edge = pack(AD, 3, False, (1,))
    LS[2, 0, 0] = line(edge, 1)
    start(l3)
    stiff((4,))
    forces((3,), adjoint_out)
    TS[2, 0] = edge + pack(AD, 3, False, (2, 3, 4))
    start(t3)
    start(f3)
    send_sum(2, take_sum(1))

    def last(xs):
        def body(g, carry):
            base = pl.multiple_of(8 + 8 * g, 8)
            rows = pl.ds(base, 8)
            own = pl.ds(pl.multiple_of(8 * g, 8), 8)
            for lt in range(2):
                low = y_sums(xs[0] + 1, lt, base)
                for x in xs:
                    high = y_sums(x + 2, lt, base)
                    e = strain6(gradients(low, high))
                    low = high
                    dot = e[0] * S0[0, x, lt, own, :]
                    for i in range(1, 6):
                        dot = dot + e[i] * S0[i, x, lt, own, :]
                    d = U[3, x + 1, lt, rows, :]
                    slope = jnp.where(MT[x, lt, own, :] == 1, 3.0 * (d * d), 0.0)
                    sens_out[x, lt, own, :] = SE[x, lt, own, :] - slope * dot
            return carry
        lax.fori_loop(0, 4, body, 0)

    arrive(t3)
    arrive(f3)
    merge(2, 2, False)
    sweep_z(AD, range(1, 5))
    last((0, 1, 2))
    arrive(l3)
    arrive(x3)
    merge(2, 2, True)
    sweep_z(AD, (5,))
    last((3,))
    sum_out[...] = take_sum(2)
    for copies in (t1, l1, f1, x1, t2, l2, f2, x2, t3, l3, f3, x3):
        left(copies)
    for stage in range(3):
        for c in ring(stage):
            c.wait_send()


def finish_kernel(count, adj, sens, total, adj_out, sens_out):
    mean = jnp.full((8, 128), jnp.sum(total[...]) * (1.0 / count) + SHIFT, F32)
    scale = (jnp.sqrt(jnp.sqrt(jnp.sqrt(mean))) / mean * (1.0 / BOOST))[0:1]
    for x in range(4):
        for lt in range(2):
            cols = slice(128 * lt, 128 * lt + 128)
            sens_out[x, :, cols] = sens[x, lt] * scale
            for c in range(3):
                adj_out[c, x, :, cols] = adj[c, x, lt] * scale


def solution(mesh):
    sizes = tuple(mesh.shape[a] for a in ("gx", "gy", "gz"))
    peers = sum(sizes) - 3
    count = sizes[0] * sizes[1] * sizes[2] * 4 * 32 * 256

    def per_device(displacement, density, material, fixed_mask):
        dma = pltpu.SemaphoreType.DMA
        vmem = pl.BlockSpec(memory_space=pltpu.VMEM)
        both = lambda n: [dma((n,)), dma((n,))]
        adj, sens, total = pl.pallas_call(
            functools.partial(kernel, sizes),
            out_shape=(jax.ShapeDtypeStruct((3, 4, 2, 32, 128), F32), jax.ShapeDtypeStruct((4, 2, 32, 128), F32),
                       jax.ShapeDtypeStruct((8, 128), F32)),
            in_specs=[pl.BlockSpec(memory_space=pl.ANY)] * 4,
            out_specs=[vmem] * 3,
            scratch_shapes=[
                pltpu.VMEM((4, 6, 2, ROWS, 128), F32),
                pltpu.VMEM((3, 6, 2, ROWS, 128), F32),
                pltpu.VMEM((3, 6, 2, ROWS, 128), F32),
                pltpu.VMEM((4, 2, 32, 128), F32),
                pltpu.VMEM((4, 2, 32, 128), jnp.int32),
                pltpu.VMEM((4, 2, 32, 128), jnp.int32),
                pltpu.VMEM((3, 6, 2, ROWS, 128), F32),
                pltpu.VMEM((3, 6, 2, ROWS, 128), F32),
                pltpu.VMEM((6, 5, 2, ROWS, 128), F32),
                pltpu.VMEM((5, 2, ROWS, 128), F32),
                pltpu.VMEM((6, 4, 2, 32, 128), F32),
                pltpu.VMEM((4, 2, 32, 128), F32),
                pltpu.VMEM((4, 2, 32, 128), F32),
                pltpu.VMEM((3, 2, 8, 128), F32),
                pltpu.VMEM((3, 2, 2, 1, 128), F32),
                pltpu.VMEM((3, 3, 3, 8, 128), F32),
                pltpu.VMEM((3, 3, 2, 3, 1, 128), F32),
                pltpu.VMEM((3, ROWS, 128), F32),
                pltpu.VMEM((7, ROWS, 128), F32),
                pltpu.VMEM((4, 32, 128), F32),
                pltpu.VMEM((3, 8, 8, 128), F32),
                dma((8,)),
                *both(8), *both(8), *both(18),
                *both(8), *both(8), *both(18),
                *both(3), *both(2), *both(2),
                *both(peers),
            ],
            compiler_params=pltpu.CompilerParams(collective_id=0, has_side_effects=True),
        )(displacement, density, material, fixed_mask)
        return pl.pallas_call(
            functools.partial(finish_kernel, count),
            out_shape=(jax.ShapeDtypeStruct((3, 4, 32, 256), F32), jax.ShapeDtypeStruct((4, 32, 256), F32)),
            in_specs=[vmem] * 3,
            out_specs=[vmem] * 2,
        )(adj, sens, total)

    placed = (P(None, "gx", "gy", "gz"), P("gx", "gy", "gz"), P("gx", "gy", "gz"), P("gx", "gy", "gz"))
    return jax.shard_map(per_device, mesh=mesh, in_specs=placed, out_specs=(placed[0], placed[1]), check_vma=False)
```

```python
import functools
import itertools

import jax
import jax.numpy as jnp
from jax import lax
from jax.experimental import pallas as pl
from jax.experimental.pallas import tpu as pltpu
from jax.sharding import PartitionSpec as P

LAM = 0.577
MU = 0.385
DIAG = (0.577 + 4.0 * 0.385) / 16.0
RELAX = 0.6
SHIFT = 1e-06
BOOST = 2.0**18
MESH = pl.DeviceIdType.MESH
ROUTE = (0, 1, 2)
ORDER = (0, 1, 2)
F32 = jnp.float32
ROWS = 48
NEAR = [d for d in itertools.product((-1, 0, 1), repeat=3) if d != (0, 0, 0)]
SIDES = [d for d in itertools.product((-1, 0, 1), repeat=2) if d != (0, 0)]
TILES = [d for d in NEAR if d[0] == 0]
LINES = [d for d in NEAR if d[0] != 0]
LAST_TILES = [(0, 0, -1), (0, -1, -1)]
OUTSIDE = (0.0, 0.0, 0.0, -1.0, 1.0)


def span(step):
    return {1: (slice(4, 6), slice(0, 2)), -1: (slice(2, 5), slice(6, 9)), 0: (slice(2, 6), slice(2, 6))}[step]


def rows_of(step):
    return {1: (slice(39, 40), slice(7, 8)), -1: (slice(8, 9), slice(40, 41)), 0: (slice(8, 40), slice(8, 40))}[step]


def kernel(sizes, disp, dens, mat, fix, adj_out, sens_out, sum_out, *scratch):
    (U, FI, AD, DN, MT, FX, PS, QS, R6, KF, S0, SE, FD, TS, LS, TR, LR, PL, PK, WP, SUM, SUM2, ST, in_sem,
     xs_, xr_, hs_, hr_, f1s, f1r, t1s, t1r, l1s, l1r, f2s, f2r, t2s, t2r, f3s, f3r, t3s, t3r, ass, asr) = scratch
    nx, ny, nz = sizes
    me = (lax.axis_index("gx"), lax.axis_index("gy"), lax.axis_index("gz"))
    lane = lax.broadcasted_iota(jnp.int32, (8, 128), 1)
    sub = lax.broadcasted_iota(jnp.int32, (8, 128), 0)
    first_lane = lane == 0
    last_lane = lane == 127

    def exists(step):
        ok = None
        for i, s, n in zip(me, step, sizes):
            if s:
                one = i < n - 1 if s > 0 else i > 0
                ok = one if ok is None else jnp.logical_and(ok, one)
        return ok

    def at(step):
        return tuple(i + s for i, s in zip(me, step))

    def back(step):
        return tuple(-s for s in step)

    barrier = pltpu.get_barrier_semaphore()

    def greet(device):
        pl.semaphore_signal(barrier, inc=1, device_id=device, device_id_type=MESH)

    place = (me[2], me[0] * ny + me[1])
    rings = []
    for k in range(1, nz):
        rings.append((0, (me[0], me[1], lax.rem(me[2] + k, nz))))
    for k in range(1, nx * ny):
        other = lax.rem(place[1] + k, nx * ny)
        rings.append((1, (other // ny, lax.rem(other, ny), me[2])))
    for _, peer in rings:
        greet(peer)
    for step in NEAR:
        pl.when(exists(step))(functools.partial(greet, at(step)))

    loads = []
    for lt in range(2):
        cols = pl.ds(lt * 128, 128)
        loads.append(pltpu.make_async_copy(disp.at[:, :, :, cols], U.at[0:3, 2:6, lt, 8:40, :], in_sem.at[4 * lt]))
        loads.append(pltpu.make_async_copy(dens.at[:, :, cols], DN.at[:, lt], in_sem.at[4 * lt + 1]))
        loads.append(pltpu.make_async_copy(mat.at[:, :, cols], MT.at[:, lt], in_sem.at[4 * lt + 2]))
        loads.append(pltpu.make_async_copy(fix.at[:, :, cols], FX.at[:, lt], in_sem.at[4 * lt + 3]))
    for c in loads:
        c.start()

    def plane_of(step):
        return 1 - step[2]

    def clear(k, ref, comps):
        for step, row in (((0, -1, 0), 7), ((0, 1, 0), 40)):
            def fill(row=row):
                for c in range(comps):
                    for x in range(9):
                        for lt in range(2):
                            ref[c, x, lt, row : row + 1, :] = jnp.full((1, 128), OUTSIDE[c], F32)
            pl.when(jnp.logical_not(exists(step)))(fill)
        for step in TILES:
            def fill(step=step):
                TR[k, plane_of(step), step[1] + 1] = outside
            pl.when(jnp.logical_not(exists(back(step))))(fill)

    outside = jnp.where(lane % 4 == 3, -1.0, 0.0)
    for step, planes in (((-1, 0, 0), (0, 1)), ((1, 0, 0), (6, 7, 8))):
        def fill(planes=planes):
            for c in range(5):
                for x in planes:
                    for lt in range(2):
                        U[c, x, lt, 7:41, :] = jnp.full((34, 128), OUTSIDE[c], F32)
        pl.when(jnp.logical_not(exists(step)))(fill)
    for step in LINES:
        def fill(step=step):
            for i in range(3):
                LR[plane_of(step), (1 - step[0]) // 2, step[1] + 1, i] = outside[0:1]
        pl.when(jnp.logical_not(exists(back(step))))(fill)
    clear(0, U, 4)
    clear(1, FI, 3)
    clear(2, AD, 3)
    for c in loads:
        c.wait()

    for x in range(4):
        for lt in range(2):
            m = MT[x, lt]
            U[3, x + 2, lt, 8:40, :] = jnp.where(m == 1, DN[x, lt], jnp.where(m == 2, 1.0, 0.0))
            U[4, x + 2, lt, 8:40, :] = FX[x, lt].astype(F32)

    def pack(ref, comps, high, xs):
        lt, source = (1, 127) if high else (0, 0)
        parts = []
        for g in range(4):
            part = jnp.zeros((8, 128), F32)
            for c in range(comps):
                for x in xs:
                    to = 32 * g + 4 * x + c
                    v = ref[c, x, lt, 8 + 8 * g : 16 + 8 * g, :]
                    part = jnp.where(lane == to, pltpu.roll(v, (to - source) % 128, 1), part)
            parts.append(part)
        return (parts[0] + parts[1]) + (parts[2] + parts[3])

    def line(tile, x):
        out = jnp.zeros((8, 128), F32)
        mine = (lane % 32) // 4 == 7 - sub
        for i in range(8):
            out = jnp.where(jnp.logical_and(mine, sub == i), pltpu.roll(tile, (28 - 4 * i - 4 * x) % 128, 1), out)
        return jnp.sum(out, axis=0, keepdims=True)

    def spread(row, x):
        moved = pltpu.roll(jnp.broadcast_to(row, (8, 128)), 0, 1, stride=4, stride_axis=0)
        return pltpu.roll(moved, (100 + 4 * x) % 128, 1)

    def remote(src, dst, send, recv, step):
        return (step, pltpu.make_async_remote_copy(
            src_ref=src, dst_ref=dst, send_sem=send, recv_sem=recv, device_id=at(step), device_id_type=MESH))

    def sides(ref, steps, comps, planes, send, recv):
        out = []
        for i, (dx, dy) in enumerate(steps):
            (sx, tx), (sr, tr) = span(dx) if dx else (planes, planes), rows_of(dy)
            out.append(remote(ref.at[0:comps, sx, :, sr, :], ref.at[0:comps, tx, :, tr, :], send.at[i], recv.at[i], (dx, dy, 0)))
        return out

    def tiles(k, steps, send, recv):
        return [remote(TS.at[k, 1 if step[2] > 0 else 0], TR.at[k, plane_of(step), step[1] + 1], send.at[i], recv.at[i], step)
                for i, step in enumerate(steps)]

    def lines(steps, send, recv):
        out = []
        for i, step in enumerate(steps):
            planes, count, side = (slice(2, 4), 2, 0) if step[0] > 0 else (slice(0, 3), 3, 1)
            out.append(remote(LS.at[1 if step[2] > 0 else 0, planes], LR.at[plane_of(step), side, step[1] + 1, 0:count],
                              send.at[i], recv.at[i], step))
        return out

    middle = nx // 2
    own = slice(8, 40)

    def plane_copy(comps, src, dst, i, step):
        return remote(U.at[comps, src, :, own, :], U.at[comps, dst, :, own, :], xs_.at[i], xr_.at[i], step)

    wide = [plane_copy(slice(0, 3), slice(4, 6), slice(0, 2), 0, (1, 0, 0)), plane_copy(slice(0, 3), slice(2, 5), slice(6, 9), 1, (-1, 0, 0))]
    thin = [plane_copy(slice(3, 5), slice(4, 6), slice(0, 2), 2, (1, 0, 0)), plane_copy(slice(3, 5), slice(2, 4), slice(6, 8), 3, (-1, 0, 0))]
    low_side, high_side = me[0] == middle - 1, me[0] == middle

    def plain(step):
        return jnp.logical_and(exists(step), jnp.logical_not(low_side if step[0] > 0 else high_side))

    def hop(c, up, leg):
        count = 2 if up else 3
        src = U.at[c, slice(4, 6) if up else slice(2, 5), :, own, :]
        dst = U.at[c, slice(0, 2) if up else slice(6, 9), :, own, :]
        stage = ST.at[c, 0:count]
        if leg == 0:
            pair, to = (src, stage), relay_of(c, up)
        else:
            pair, to = (src if ROUTE[c] is None else stage, dst), (middle if up else middle - 1)
        i = (2 * c + (0 if up else 1)) * 2 + leg
        return pltpu.make_async_remote_copy(src_ref=pair[0], dst_ref=pair[1], send_sem=hs_.at[i], recv_sem=hr_.at[i],
                                            device_id=(to, me[1], me[2]), device_id_type=MESH)

    def relay_of(c, up):
        return ROUTE[c] if up else nx - 1 - ROUTE[c]

    crossings = [(c, up, low_side if up else high_side, high_side if up else low_side) for c in ORDER for up in (True, False)]

    def send_across():
        for c, up, here, _ in crossings:
            pl.when(here)(hop(c, up, 1 if ROUTE[c] is None else 0).start)

    def send_planes():
        for step, c in wide:
            pl.when(plain(step))(c.start)

    def relay_planes():
        for c, up, _, _ in crossings:
            if ROUTE[c] is not None:
                def forward(c=c, up=up):
                    hop(c, up, 0).wait_recv()
                    hop(c, up, 1).start()
                pl.when(me[0] == relay_of(c, up))(forward)

    def arrive_planes():
        arrive(thin)
        for step, c in wide:
            pl.when(plain(back(step)))(c.wait_recv)
        for c, up, _, there in crossings:
            pl.when(there)(hop(c, up, 1).wait_recv)

    def left_planes():
        left(thin)
        for step, c in wide:
            pl.when(plain(step))(c.wait_send)
        for c, up, here, _ in crossings:
            if ROUTE[c] is None:
                pl.when(here)(hop(c, up, 1).wait_send)
            else:
                pl.when(here)(hop(c, up, 0).wait_send)
                pl.when(me[0] == relay_of(c, up))(hop(c, up, 1).wait_send)

    def along(copies):
        return [c for c in copies if c[0][0] == 0], [c for c in copies if c[0][0] != 0]

    def start(copies):
        for step, c in copies:
            pl.when(exists(step))(c.start)

    def arrive(copies):
        for step, c in copies:
            pl.when(exists(back(step)))(c.wait_recv)

    def left(copies):
        for step, c in copies:
            pl.when(exists(step))(c.wait_send)

    def merge(k, plane, with_x):
        for dy in (-1, 0, 1):
            full = TS[k, 0] if plane == 1 and dy == 0 else TR[k, plane, dy + 1]
            if with_x:
                for side, i, x in ((0, 0, 0), (0, 1, 1), (1, 0, 6), (1, 1, 7)):
                    here = jnp.logical_and(lane % 32 >= 4 * x, lane % 32 < 4 * x + 4)
                    full = jnp.where(here, spread(LR[plane, side, dy + 1, i], x), full)
                far = spread(LR[plane, 1, dy + 1, 2], 0)

            def unfold(shift):
                part = pltpu.roll(full, shift, 1) if shift else full
                if with_x:
                    part = jnp.where(jnp.logical_and(lane >= 32, lane < 36), pltpu.roll(far, (shift + 32) % 128, 1), part)
                return part

            if dy == 0:
                for g in range(4):
                    PL[plane, 8 + 8 * g : 16 + 8 * g, :] = unfold((128 - 32 * g) % 128)
            elif dy == 1:
                PL[plane, 0:8, :] = unfold(32)
            else:
                PL[plane, 40:48, :] = unfold(0)

    def sweep_z(ref, xs):
        def body(g, carry):
            rows = pl.ds(7 + 8 * g, 8)
            edge = PL[2, rows, :]
            for c in range(3):
                for x in xs:
                    t0, t1 = ref[c, x, 0, rows, :], ref[c, x, 1, rows, :]
                    r0, r1 = pltpu.roll(t0, 127, 1), pltpu.roll(t1, 127, 1)
                    s0 = jnp.where(last_lane, r1, r0)
                    s1 = jnp.where(last_lane, pltpu.roll(edge, 127 - 4 * x - c, 1), r1)
                    PS[c, x, 0, rows, :] = s0 + t0
                    PS[c, x, 1, rows, :] = s1 + t1
                    QS[c, x, 0, rows, :] = s0 - t0
                    QS[c, x, 1, rows, :] = s1 - t1
            return carry
        lax.fori_loop(0, 5, body, 0)

    def gradients(low, high):
        return [[high[c][0] - low[c][0] for c in range(3)], [high[c][1] + low[c][1] for c in range(3)],
                [high[c][2] + low[c][2] for c in range(3)]]

    def strain6(g):
        gx, gy, gz = g
        return gx[0], gy[1], gz[2], gy[0] + gx[1], gz[1] + gy[2], gx[2] + gz[0]

    def y_sums(x, lt, base):
        out = []
        for c in range(3):
            p0, p1 = PS[c, x, lt, pl.ds(base, 8), :], PS[c, x, lt, pl.ds(base + 1, 8), :]
            q0, q1 = QS[c, x, lt, pl.ds(base, 8), :], QS[c, x, lt, pl.ds(base + 1, 8), :]
            out.append((p0 + p1, p1 - p0, q0 + q1))
        return out

    def packed_strain():
        lo, hi = PL[0], PL[1]
        PK[0] = lo + hi
        PK[1] = hi - lo
        p0, p1, q0, q1 = PK[0, 0:40], PK[0, 1:41], PK[1, 0:40], PK[1, 1:41]
        a, b, c = p0 + p1, p1 - p0, q0 + q1
        g = [pltpu.roll(a, 124, 1) - a, pltpu.roll(b, 124, 1) + b, pltpu.roll(c, 124, 1) + c]
        return strain6([[t] + [pltpu.roll(t, 128 - i, 1) for i in (1, 2)] for t in g])

    def stiffness(d):
        return jnp.where(d < 0.0, 0.0, 0.001 + d * d * d)

    def load_terms(e, d):
        a, b, c = e[0] - e[1], e[1] - e[2], e[2] - e[0]
        q = (MU * MU / 16.0) * (2.0 * (a * a + b * b + c * c) + 3.0 * (e[3] * e[3] + e[4] * e[4] + e[5] * e[5]))
        vm = d * q
        w = vm * vm * vm
        t = (-MU * MU / 8.0 * BOOST) * (w * d)
        ts = 1.5 * t
        return q, vm, w, (t * (a - c), t * (b - a), t * (c - b), ts * e[3], ts * e[4], ts * e[5])

    def stiff_terms(e, kf):
        k = kf * (-2.0 * MU / 16.0)
        tr = (kf * (-LAM / 16.0)) * (e[0] + e[1] + e[2])
        ks = kf * (-MU / 16.0)
        return tr + k * e[0], tr + k * e[1], tr + k * e[2], ks * e[3], ks * e[4], ks * e[5]

    S_Y, D_Y = (0, 3, 5, 4, 2), (3, 1, 4)

    def x_parts(low, high):
        (sl, dl), (sh, dh) = low, high
        return [((sh[i] - sl[i]) + (dh[j] + dl[j]), sh[k] + sl[k]) for i, j, k in ((0, 3, 5), (3, 1, 4), (5, 4, 2))]

    def packed_forces(r):
        for i in range(6):
            PK[i, 0:40] = r[i]
        s = {i: PK[i, 7:39] + PK[i, 8:40] for i in S_Y}
        d = {i: PK[i, 8:40] - PK[i, 7:39] for i in D_Y}
        high = ({i: pltpu.roll(v, 124, 1) for i, v in s.items()}, {i: pltpu.roll(v, 124, 1) for i, v in d.items()})
        for c, (u, w) in enumerate(x_parts((s, d), high)):
            WP[c] = u - w

    def from_low(w0, w1, packed, x):
        r0, r1 = pltpu.roll(w0, 1, 1), pltpu.roll(w1, 1, 1)
        edge = pltpu.roll(packed, 132 - 4 * x, 1) if x > 1 else packed
        return jnp.where(first_lane, edge, r0), jnp.where(first_lane, r0, r1)

    def forces(xs, finish):
        def body(g, carry):
            base = pl.multiple_of(8 + 8 * g, 8)
            own = pl.ds(pl.multiple_of(8 * g, 8), 8)
            packed = [WP[c, own, :] for c in range(3)]

            def sums(x):
                out = []
                for lt in range(2):
                    r1 = [R6[i, x, lt, pl.ds(base, 8), :] for i in range(6)]
                    r0 = [R6[i, x, lt, pl.ds(base - 1, 8), :] for i in range(6)]
                    out.append(({i: r0[i] + r1[i] for i in S_Y}, {i: r1[i] - r0[i] for i in D_Y}))
                return out

            low = sums(xs[0] - 1)
            for x in xs:
                high = sums(x)
                p0, p1 = x_parts(low[0], high[0]), x_parts(low[1], high[1])
                for c in range(3):
                    (u0, c0), (u1, c1) = p0[c], p1[c]
                    s0, s1 = from_low(u0 - c0, u1 - c1, packed[c], x)
                    finish(c, x, 0, base, own, u0 + c0 + s0)
                    finish(c, x, 1, base, own, u1 + c1 + s1)
                low = high
            return carry
        lax.fori_loop(0, 4, body, 0)

    TS[0, 0] = pack(U, 4, False, range(2, 6))
    TS[0, 1] = pack(U, 4, True, range(2, 6))
    for z in range(2):
        for x in range(4):
            LS[z, x] = line(TS[0, z], x + 2)

    t1 = tiles(0, TILES, t1s, t1r)
    l1 = lines(LINES, l1s, l1r)
    f1, x1 = along(sides(U, [d for d in SIDES if d[1]], 4, slice(2, 6), f1s, f1r))
    t2 = tiles(1, TILES, t2s, t2r)
    f2 = sides(FI, [(0, 1), (0, -1)], 3, slice(1, 8), f2s, f2r)
    t3 = tiles(2, LAST_TILES, t3s, t3r)
    f3 = sides(AD, [(0, -1)], 3, slice(2, 7), f3s, f3r)

    block = 1
    for i, n in zip(me, sizes):
        block = block * (1 + (i > 0).astype(jnp.int32) + (i < n - 1).astype(jnp.int32))
    pl.semaphore_wait(barrier, block - 1 + len(rings))

    send_across()
    start(l1)
    start(x1)
    start(t1)
    start(f1)
    start(thin)
    send_planes()
    relay_planes()

    def power(xs, total):
        def body(g, total):
            base = pl.multiple_of(8 * g, 8)
            rows = pl.ds(base, 8)
            own = pl.ds(pl.multiple_of(jnp.maximum(8 * g - 8, 0), 8), 8)
            inside = jnp.full((8, 128), g, jnp.int32) > 0
            for lt in range(2):
                low = y_sums(xs[0], lt, base)
                for x in xs:
                    high = y_sums(x + 1, lt, base)
                    e = strain6(gradients(low, high))
                    low = high
                    q, vm, w, r = load_terms(e, jnp.maximum(U[3, x, lt, rows, :], 0.0))
                    for i in range(6):
                        R6[i, x, lt, rows, :] = r[i]
                    if 2 <= x < 6:
                        v2 = vm * vm
                        total = total + jnp.where(inside, v2 * v2, 0.0)
                        tr = (LAM / 16.0) * (e[0] + e[1] + e[2])
                        for i in range(6):
                            S0[i, x - 2, lt, own, :] = tr + (MU / 8.0) * e[i] if i < 3 else (MU / 16.0) * e[i]
                        SE[x - 2, lt, own, :] = jnp.where(MT[x - 2, lt, own, :] == 1, (0.5 * BOOST) * (w * q), 0.0)
            return total
        return lax.fori_loop(0, 5, body, total)

    def fill_stiffness(xs):
        for x in xs:
            for lt in range(2):
                KF[x, lt, 0:40, :] = stiffness(U[3, x, lt, 0:40, :])

    def packed_load():
        d = pltpu.roll(PL[0, 0:40, :], 125, 1)
        kp = stiffness(d)
        packed_forces(load_terms(packed_strain(), jnp.maximum(d, 0.0))[3])
        PK[6, 0:40] = kp
        ky = PK[6, 7:39] + PK[6, 8:40]
        WP[3] = ky + pltpu.roll(ky, 124, 1)

    def diagonal(xs):
        def body(g, carry):
            base = pl.multiple_of(8 + 8 * g, 8)
            own = pl.ds(pl.multiple_of(8 * g, 8), 8)
            packed = WP[3, own, :]

            def sums(x):
                return [KF[x, lt, pl.ds(base, 8), :] + KF[x, lt, pl.ds(base - 1, 8), :] for lt in range(2)]

            low = sums(xs[0] - 1)
            for x in xs:
                high = sums(x)
                k0, k1 = low[0] + high[0], low[1] + high[1]
                s0, s1 = from_low(k0, k1, packed, x)
                for lt, k in ((0, k0 + s0), (1, k1 + s1)):
                    fixed = U[4, x, lt, pl.ds(base, 8), :]
                    FD[x, lt, own, :] = (1.0 - fixed) / (DIAG * k + fixed)
                low = high
            return carry
        lax.fori_loop(0, 4, body, 0)

    def first_out(c, x, lt, base, own, value):
        FI[c, x, lt, pl.ds(base, 8), :] = value * FD[x, lt, own, :]

    def ring(stage):
        buf = SUM if stage == 0 else SUM2
        return [pltpu.make_async_remote_copy(
            src_ref=buf.at[place[stage]], dst_ref=buf.at[place[stage]],
            send_sem=ass.at[i], recv_sem=asr.at[i], device_id=peer, device_id_type=MESH)
            for i, (a, peer) in enumerate(rings) if a == stage]

    def send_sum(stage, value):
        (SUM if stage == 0 else SUM2)[place[stage]] = value
        for c in ring(stage):
            c.start()

    def take_sum(stage):
        for c in ring(stage):
            c.wait_recv()
        buf, n = (SUM, nz) if stage == 0 else (SUM2, nx * ny)
        value = buf[0]
        for i in range(1, n):
            value = value + buf[i]
        return value

    arrive(t1)
    arrive(f1)
    for plane in range(3):
        merge(0, plane, False)
    packed_load()
    sweep_z(U, range(2, 6))
    total = power((2, 3, 4), jnp.zeros((8, 128), F32))
    fill_stiffness(range(2, 6))
    diagonal((3, 4, 5))
    forces((3, 4), first_out)

    arrive(l1)
    arrive(x1)
    for plane in range(3):
        merge(0, plane, True)
    packed_load()
    arrive_planes()
    sweep_z(U, (0, 1, 6, 7, 8))
    fill_stiffness((0, 1, 6, 7))
    diagonal((1, 2))
    diagonal((6, 7))
    total = power((5, 6, 7), total)
    send_sum(0, jnp.sum(total, axis=0, keepdims=True))
    power((0, 1), total)
    forces((1, 2), first_out)
    forces((5, 6, 7), first_out)
    start(f2)
    TS[1, 0] = pack(FI, 3, False, range(1, 8))
    TS[1, 1] = pack(FI, 3, True, range(1, 8))
    start(t2)
    send_sum(1, take_sum(0))

    def stiff(xs):
        def body(g, carry):
            base = pl.multiple_of(8 * g, 8)
            rows = pl.ds(base, 8)
            for lt in range(2):
                low = y_sums(xs[0], lt, base)
                for x in xs:
                    high = y_sums(x + 1, lt, base)
                    r = stiff_terms(strain6(gradients(low, high)), KF[x, lt, rows, :])
                    low = high
                    for i in range(6):
                        R6[i, x, lt, rows, :] = r[i]
            return carry
        lax.fori_loop(0, 5, body, 0)

    def packed_stiff():
        packed_forces(stiff_terms(packed_strain(), kp_ref[...]))

    def adjoint_out(c, x, lt, base, own, value):
        new = (1.0 + RELAX) * FI[c, x, lt, pl.ds(base, 8), :] - RELAX * FD[x, lt, own, :] * value
        AD[c, x, lt, pl.ds(base, 8), :] = new
        if x < 6:
            adj_out[c, x - 2, lt, own, :] = new

    kp_ref = PK.at[6, 0:40]
    arrive(t2)
    arrive(f2)
    for plane in range(3):
        merge(1, plane, False)
    packed_stiff()
    sweep_z(FI, range(1, 8))
    stiff(range(1, 7))
    forces(range(2, 7), adjoint_out)
    start(f3)
    TS[2, 0] = pack(AD, 3, False, range(2, 7))
    start(t3)

    def last(xs):
        def body(g, carry):
            base = pl.multiple_of(8 + 8 * g, 8)
            rows = pl.ds(base, 8)
            own = pl.ds(pl.multiple_of(8 * g, 8), 8)
            for lt in range(2):
                low = y_sums(xs[0] + 2, lt, base)
                for x in xs:
                    high = y_sums(x + 3, lt, base)
                    e = strain6(gradients(low, high))
                    low = high
                    dot = e[0] * S0[0, x, lt, own, :]
                    for i in range(1, 6):
                        dot = dot + e[i] * S0[i, x, lt, own, :]
                    d = U[3, x + 2, lt, rows, :]
                    slope = jnp.where(MT[x, lt, own, :] == 1, 3.0 * (d * d), 0.0)
                    sens_out[x, lt, own, :] = SE[x, lt, own, :] - slope * dot
            return carry
        lax.fori_loop(0, 4, body, 0)

    arrive(t3)
    arrive(f3)
    merge(2, 2, False)
    sweep_z(AD, range(2, 7))
    last((0, 1, 2, 3))
    sum_out[...] = take_sum(1)
    left_planes()
    for copies in (t1, l1, f1, x1, t2, f2, t3, f3):
        left(copies)
    for stage in range(2):
        for c in ring(stage):
            c.wait_send()


def finish_kernel(count, adj, sens, total, adj_out, sens_out):
    mean = jnp.full((8, 128), jnp.sum(total[...]) * (1.0 / count) + SHIFT, F32)
    scale = (jnp.sqrt(jnp.sqrt(jnp.sqrt(mean))) / mean * (1.0 / BOOST))[0:1]
    for x in range(4):
        for lt in range(2):
            cols = slice(128 * lt, 128 * lt + 128)
            sens_out[x, :, cols] = sens[x, lt] * scale
            for c in range(3):
                adj_out[c, x, :, cols] = adj[c, x, lt] * scale


def solution(mesh):
    sizes = tuple(mesh.shape[a] for a in ("gx", "gy", "gz"))
    peers = sizes[2] - 1 + sizes[0] * sizes[1] - 1
    count = sizes[0] * sizes[1] * sizes[2] * 4 * 32 * 256

    def per_device(displacement, density, material, fixed_mask):
        dma = pltpu.SemaphoreType.DMA
        vmem = pl.BlockSpec(memory_space=pltpu.VMEM)
        both = lambda n: [dma((n,)), dma((n,))]
        adj, sens, total = pl.pallas_call(
            functools.partial(kernel, sizes),
            out_shape=(jax.ShapeDtypeStruct((3, 4, 2, 32, 128), F32), jax.ShapeDtypeStruct((4, 2, 32, 128), F32),
                       jax.ShapeDtypeStruct((1, 128), F32)),
            in_specs=[pl.BlockSpec(memory_space=pl.ANY)] * 4,
            out_specs=[vmem] * 3,
            scratch_shapes=[
                pltpu.VMEM((5, 9, 2, ROWS, 128), F32),
                pltpu.VMEM((3, 9, 2, ROWS, 128), F32),
                pltpu.VMEM((3, 9, 2, ROWS, 128), F32),
                pltpu.VMEM((4, 2, 32, 128), F32),
                pltpu.VMEM((4, 2, 32, 128), jnp.int32),
                pltpu.VMEM((4, 2, 32, 128), jnp.int32),
                pltpu.VMEM((3, 9, 2, ROWS, 128), F32),
                pltpu.VMEM((3, 9, 2, ROWS, 128), F32),
                pltpu.VMEM((6, 8, 2, ROWS, 128), F32),
                pltpu.VMEM((8, 2, ROWS, 128), F32),
                pltpu.VMEM((6, 4, 2, 32, 128), F32),
                pltpu.VMEM((4, 2, 32, 128), F32),
                pltpu.VMEM((8, 2, 32, 128), F32),
                pltpu.VMEM((3, 2, 8, 128), F32),
                pltpu.VMEM((2, 4, 1, 128), F32),
                pltpu.VMEM((3, 3, 3, 8, 128), F32),
                pltpu.VMEM((3, 2, 3, 3, 1, 128), F32),
                pltpu.VMEM((3, ROWS, 128), F32),
                pltpu.VMEM((7, ROWS, 128), F32),
                pltpu.VMEM((4, 32, 128), F32),
                pltpu.VMEM((sizes[2], 1, 128), F32),
                pltpu.VMEM((sizes[0] * sizes[1], 1, 128), F32),
                pltpu.VMEM((3, 3, 2, 32, 128), F32),
                dma((8,)),
                *both(4), *both(12), *both(6), *both(8), *both(18),
                *both(2), *both(8), *both(1), *both(2),
                *both(peers),
            ],
            compiler_params=pltpu.CompilerParams(collective_id=0, has_side_effects=True),
        )(displacement, density, material, fixed_mask)
        return pl.pallas_call(
            functools.partial(finish_kernel, count),
            out_shape=(jax.ShapeDtypeStruct((3, 4, 32, 256), F32), jax.ShapeDtypeStruct((4, 32, 256), F32)),
            in_specs=[vmem] * 3,
            out_specs=[vmem] * 2,
        )(adj, sens, total)

    placed = (P(None, "gx", "gy", "gz"), P("gx", "gy", "gz"), P("gx", "gy", "gz"), P("gx", "gy", "gz"))
    return jax.shard_map(per_device, mesh=mesh, in_specs=placed, out_specs=(placed[0], placed[1]), check_vma=False)
```

```python
import functools
import itertools

import jax
import jax.numpy as jnp
from jax import lax
from jax.experimental import pallas as pl
from jax.experimental.pallas import tpu as pltpu
from jax.sharding import PartitionSpec as P

LAM = 0.577
MU = 0.385
DIAG = (0.577 + 4.0 * 0.385) / 16.0
RELAX = 0.6
SHIFT = 1e-06
BOOST = 2.0**18
MESH = pl.DeviceIdType.MESH
ROUTE = (0, 1, 2)
ORDER = (0, 1, 2)
F32 = jnp.float32
ROWS = 48
NEAR = [d for d in itertools.product((-1, 0, 1), repeat=3) if d != (0, 0, 0)]
SIDES = [d for d in itertools.product((-1, 0, 1), repeat=2) if d != (0, 0)]
TILES = [d for d in NEAR if d[0] == 0]
LINES = [d for d in NEAR if d[0] != 0]
LAST_TILES = [(0, 0, -1), (0, -1, -1)]
OUTSIDE = (0.0, 0.0, 0.0, -1.0, 1.0)


def span(step):
    return {1: (slice(4, 6), slice(0, 2)), -1: (slice(2, 5), slice(6, 9)), 0: (slice(2, 6), slice(2, 6))}[step]


def rows_of(step):
    return {1: (slice(39, 40), slice(7, 8)), -1: (slice(8, 9), slice(40, 41)), 0: (slice(8, 40), slice(8, 40))}[step]


def kernel(sizes, disp, dens, mat, fix, adj_out, sens_out, sum_out, *scratch):
    (U, FI, AD, DN, MT, FX, PS, QS, R6, KF, S0, SE, FD, TS, LS, TR, LR, PL, PK, WP, SUM, SUM2, ST, in_sem,
     xs_, xr_, hs_, hr_, f1s, f1r, t1s, t1r, l1s, l1r, f2s, f2r, t2s, t2r, f3s, f3r, t3s, t3r, ass, asr) = scratch
    nx, ny, nz = sizes
    me = (lax.axis_index("gx"), lax.axis_index("gy"), lax.axis_index("gz"))
    lane = lax.broadcasted_iota(jnp.int32, (8, 128), 1)
    sub = lax.broadcasted_iota(jnp.int32, (8, 128), 0)
    first_lane = lane == 0
    last_lane = lane == 127

    def exists(step):
        ok = None
        for i, s, n in zip(me, step, sizes):
            if s:
                one = i < n - 1 if s > 0 else i > 0
                ok = one if ok is None else jnp.logical_and(ok, one)
        return ok

    def at(step):
        return tuple(i + s for i, s in zip(me, step))

    def back(step):
        return tuple(-s for s in step)

    barrier = pltpu.get_barrier_semaphore()

    def greet(device):
        pl.semaphore_signal(barrier, inc=1, device_id=device, device_id_type=MESH)

    place = (me[2], me[0] * ny + me[1])
    rings = []
    for k in range(1, nz):
        rings.append((0, (me[0], me[1], lax.rem(me[2] + k, nz))))
    for k in range(1, nx * ny):
        other = lax.rem(place[1] + k, nx * ny)
        rings.append((1, (other // ny, lax.rem(other, ny), me[2])))
    for _, peer in rings:
        greet(peer)
    for step in NEAR:
        pl.when(exists(step))(functools.partial(greet, at(step)))

    loads = []
    for lt in range(2):
        cols = pl.ds(lt * 128, 128)
        loads.append(pltpu.make_async_copy(disp.at[:, :, :, cols], U.at[0:3, 2:6, lt, 8:40, :], in_sem.at[4 * lt]))
        loads.append(pltpu.make_async_copy(dens.at[:, :, cols], DN.at[:, lt], in_sem.at[4 * lt + 1]))
        loads.append(pltpu.make_async_copy(mat.at[:, :, cols], MT.at[:, lt], in_sem.at[4 * lt + 2]))
        loads.append(pltpu.make_async_copy(fix.at[:, :, cols], FX.at[:, lt], in_sem.at[4 * lt + 3]))
    for c in loads:
        c.start()

    def plane_of(step):
        return 1 - step[2]

    def clear(k, ref, comps):
        for step, row in (((0, -1, 0), 7), ((0, 1, 0), 40)):
            def fill(row=row):
                for c in range(comps):
                    for x in range(9):
                        for lt in range(2):
                            ref[c, x, lt, row : row + 1, :] = jnp.full((1, 128), OUTSIDE[c], F32)
            pl.when(jnp.logical_not(exists(step)))(fill)
        for step in TILES:
            def fill(step=step):
                TR[k, plane_of(step), step[1] + 1] = outside
            pl.when(jnp.logical_not(exists(back(step))))(fill)

    outside = jnp.where(lane % 4 == 3, -1.0, 0.0)
    for step, planes in (((-1, 0, 0), (0, 1)), ((1, 0, 0), (6, 7, 8))):
        def fill(planes=planes):
            for c in range(5):
                for x in planes:
                    for lt in range(2):
                        U[c, x, lt, 7:41, :] = jnp.full((34, 128), OUTSIDE[c], F32)
        pl.when(jnp.logical_not(exists(step)))(fill)
    for step in LINES:
        def fill(step=step):
            for i in range(3):
                LR[plane_of(step), (1 - step[0]) // 2, step[1] + 1, i] = outside[0:1]
        pl.when(jnp.logical_not(exists(back(step))))(fill)
    clear(0, U, 4)
    clear(1, FI, 3)
    clear(2, AD, 3)
    for c in loads:
        c.wait()

    for x in range(4):
        for lt in range(2):
            m = MT[x, lt]
            U[3, x + 2, lt, 8:40, :] = jnp.where(m == 1, DN[x, lt], jnp.where(m == 2, 1.0, 0.0))
            U[4, x + 2, lt, 8:40, :] = FX[x, lt].astype(F32)

    def pack(ref, comps, high, xs):
        lt, source = (1, 127) if high else (0, 0)
        parts = []
        for g in range(4):
            part = jnp.zeros((8, 128), F32)
            for c in range(comps):
                for x in xs:
                    to = 32 * g + 4 * x + c
                    v = ref[c, x, lt, 8 + 8 * g : 16 + 8 * g, :]
                    part = jnp.where(lane == to, pltpu.roll(v, (to - source) % 128, 1), part)
            parts.append(part)
        return (parts[0] + parts[1]) + (parts[2] + parts[3])

    def line(tile, x):
        out = jnp.zeros((8, 128), F32)
        mine = (lane % 32) // 4 == 7 - sub
        for i in range(8):
            out = jnp.where(jnp.logical_and(mine, sub == i), pltpu.roll(tile, (28 - 4 * i - 4 * x) % 128, 1), out)
        return jnp.sum(out, axis=0, keepdims=True)

    def spread(row, x):
        moved = pltpu.roll(jnp.broadcast_to(row, (8, 128)), 0, 1, stride=4, stride_axis=0)
        return pltpu.roll(moved, (100 + 4 * x) % 128, 1)

    def remote(src, dst, send, recv, step):
        return (step, pltpu.make_async_remote_copy(
            src_ref=src, dst_ref=dst, send_sem=send, recv_sem=recv, device_id=at(step), device_id_type=MESH))

    def sides(ref, steps, comps, planes, send, recv):
        out = []
        for i, (dx, dy) in enumerate(steps):
            (sx, tx), (sr, tr) = span(dx) if dx else (planes, planes), rows_of(dy)
            out.append(remote(ref.at[0:comps, sx, :, sr, :], ref.at[0:comps, tx, :, tr, :], send.at[i], recv.at[i], (dx, dy, 0)))
        return out

    def tiles(k, steps, send, recv):
        return [remote(TS.at[k, 1 if step[2] > 0 else 0], TR.at[k, plane_of(step), step[1] + 1], send.at[i], recv.at[i], step)
                for i, step in enumerate(steps)]

    def lines(steps, send, recv):
        out = []
        for i, step in enumerate(steps):
            planes, count, side = (slice(2, 4), 2, 0) if step[0] > 0 else (slice(0, 3), 3, 1)
            out.append(remote(LS.at[1 if step[2] > 0 else 0, planes], LR.at[plane_of(step), side, step[1] + 1, 0:count],
                              send.at[i], recv.at[i], step))
        return out

    middle = nx // 2
    own = slice(8, 40)

    def plane_copy(comps, src, dst, i, step):
        return remote(U.at[comps, src, :, own, :], U.at[comps, dst, :, own, :], xs_.at[i], xr_.at[i], step)

    wide = [plane_copy(slice(0, 3), slice(4, 6), slice(0, 2), 0, (1, 0, 0)), plane_copy(slice(0, 3), slice(2, 5), slice(6, 9), 1, (-1, 0, 0))]
    thin = [plane_copy(slice(3, 5), slice(4, 6), slice(0, 2), 2, (1, 0, 0)), plane_copy(slice(3, 5), slice(2, 4), slice(6, 8), 3, (-1, 0, 0))]
    low_side, high_side = me[0] == middle - 1, me[0] == middle

    def plain(step):
        return jnp.logical_and(exists(step), jnp.logical_not(low_side if step[0] > 0 else high_side))

    def hop(c, up, leg):
        count = 2 if up else 3
        src = U.at[c, slice(4, 6) if up else slice(2, 5), :, own, :]
        dst = U.at[c, slice(0, 2) if up else slice(6, 9), :, own, :]
        stage = ST.at[c, 0:count]
        if leg == 0:
            pair, to = (src, stage), relay_of(c, up)
        else:
            pair, to = (src if ROUTE[c] is None else stage, dst), (middle if up else middle - 1)
        i = (2 * c + (0 if up else 1)) * 2 + leg
        return pltpu.make_async_remote_copy(src_ref=pair[0], dst_ref=pair[1], send_sem=hs_.at[i], recv_sem=hr_.at[i],
                                            device_id=(to, me[1], me[2]), device_id_type=MESH)

    def relay_of(c, up):
        return ROUTE[c] if up else nx - 1 - ROUTE[c]

    crossings = [(c, up, low_side if up else high_side, high_side if up else low_side) for c in ORDER for up in (True, False)]

    def send_across():
        for c, up, here, _ in crossings:
            pl.when(here)(hop(c, up, 1 if ROUTE[c] is None else 0).start)

    def send_planes():
        for step, c in wide:
            pl.when(plain(step))(c.start)

    def relay_planes():
        for c, up, _, _ in crossings:
            if ROUTE[c] is not None:
                def forward(c=c, up=up):
                    hop(c, up, 0).wait_recv()
                    hop(c, up, 1).start()
                pl.when(me[0] == relay_of(c, up))(forward)

    def arrive_planes():
        arrive(thin)
        for step, c in wide:
            pl.when(plain(back(step)))(c.wait_recv)
        for c, up, _, there in crossings:
            pl.when(there)(hop(c, up, 1).wait_recv)

    def left_planes():
        left(thin)
        for step, c in wide:
            pl.when(plain(step))(c.wait_send)
        for c, up, here, _ in crossings:
            if ROUTE[c] is None:
                pl.when(here)(hop(c, up, 1).wait_send)
            else:
                pl.when(here)(hop(c, up, 0).wait_send)
                pl.when(me[0] == relay_of(c, up))(hop(c, up, 1).wait_send)

    def along(copies):
        return [c for c in copies if c[0][0] == 0], [c for c in copies if c[0][0] != 0]

    def start(copies):
        for step, c in copies:
            pl.when(exists(step))(c.start)

    def arrive(copies):
        for step, c in copies:
            pl.when(exists(back(step)))(c.wait_recv)

    def left(copies):
        for step, c in copies:
            pl.when(exists(step))(c.wait_send)

    def merge(k, plane, with_x):
        for dy in (-1, 0, 1):
            full = TS[k, 0] if plane == 1 and dy == 0 else TR[k, plane, dy + 1]
            if with_x:
                for side, i, x in ((0, 0, 0), (0, 1, 1), (1, 0, 6), (1, 1, 7)):
                    here = jnp.logical_and(lane % 32 >= 4 * x, lane % 32 < 4 * x + 4)
                    full = jnp.where(here, spread(LR[plane, side, dy + 1, i], x), full)
                far = spread(LR[plane, 1, dy + 1, 2], 0)

            def unfold(shift):
                part = pltpu.roll(full, shift, 1) if shift else full
                if with_x:
                    part = jnp.where(jnp.logical_and(lane >= 32, lane < 36), pltpu.roll(far, (shift + 32) % 128, 1), part)
                return part

            if dy == 0:
                for g in range(4):
                    PL[plane, 8 + 8 * g : 16 + 8 * g, :] = unfold((128 - 32 * g) % 128)
            elif dy == 1:
                PL[plane, 0:8, :] = unfold(32)
            else:
                PL[plane, 40:48, :] = unfold(0)

    def sweep_z(ref, xs):
        def body(g, carry):
            rows = pl.ds(7 + 8 * g, 8)
            edge = PL[2, rows, :]
            for c in range(3):
                for x in xs:
                    t0, t1 = ref[c, x, 0, rows, :], ref[c, x, 1, rows, :]
                    r0, r1 = pltpu.roll(t0, 127, 1), pltpu.roll(t1, 127, 1)
                    s0 = jnp.where(last_lane, r1, r0)
                    s1 = jnp.where(last_lane, pltpu.roll(edge, 127 - 4 * x - c, 1), r1)
                    PS[c, x, 0, rows, :] = s0 + t0
                    PS[c, x, 1, rows, :] = s1 + t1
                    QS[c, x, 0, rows, :] = s0 - t0
                    QS[c, x, 1, rows, :] = s1 - t1
            return carry
        lax.fori_loop(0, 5, body, 0)

    def gradients(low, high):
        return [[high[c][0] - low[c][0] for c in range(3)], [high[c][1] + low[c][1] for c in range(3)],
                [high[c][2] + low[c][2] for c in range(3)]]

    def strain6(g):
        gx, gy, gz = g
        return gx[0], gy[1], gz[2], gy[0] + gx[1], gz[1] + gy[2], gx[2] + gz[0]

    def y_sums(x, lt, base):
        out = []
        for c in range(3):
            p0, p1 = PS[c, x, lt, pl.ds(base, 8), :], PS[c, x, lt, pl.ds(base + 1, 8), :]
            q0, q1 = QS[c, x, lt, pl.ds(base, 8), :], QS[c, x, lt, pl.ds(base + 1, 8), :]
            out.append((p0 + p1, p1 - p0, q0 + q1))
        return out

    def packed_strain():
        lo, hi = PL[0], PL[1]
        PK[0] = lo + hi
        PK[1] = hi - lo
        p0, p1, q0, q1 = PK[0, 0:40], PK[0, 1:41], PK[1, 0:40], PK[1, 1:41]
        a, b, c = p0 + p1, p1 - p0, q0 + q1
        g = [pltpu.roll(a, 124, 1) - a, pltpu.roll(b, 124, 1) + b, pltpu.roll(c, 124, 1) + c]
        return strain6([[t] + [pltpu.roll(t, 128 - i, 1) for i in (1, 2)] for t in g])

    def stiffness(d):
        return jnp.where(d < 0.0, 0.0, 0.001 + d * d * d)

    def load_terms(e, d):
        a, b, c = e[0] - e[1], e[1] - e[2], e[2] - e[0]
        q = (MU * MU / 16.0) * (2.0 * (a * a + b * b + c * c) + 3.0 * (e[3] * e[3] + e[4] * e[4] + e[5] * e[5]))
        vm = d * q
        w = vm * vm * vm
        t = (-MU * MU / 8.0 * BOOST) * (w * d)
        ts = 1.5 * t
        return q, vm, w, (t * (a - c), t * (b - a), t * (c - b), ts * e[3], ts * e[4], ts * e[5])

    def stiff_terms(e, kf):
        k = kf * (-2.0 * MU / 16.0)
        tr = (kf * (-LAM / 16.0)) * (e[0] + e[1] + e[2])
        ks = kf * (-MU / 16.0)
        return tr + k * e[0], tr + k * e[1], tr + k * e[2], ks * e[3], ks * e[4], ks * e[5]

    S_Y, D_Y = (0, 3, 5, 4, 2), (3, 1, 4)

    def x_parts(low, high):
        (sl, dl), (sh, dh) = low, high
        return [((sh[i] - sl[i]) + (dh[j] + dl[j]), sh[k] + sl[k]) for i, j, k in ((0, 3, 5), (3, 1, 4), (5, 4, 2))]

    def packed_forces(r):
        for i in range(6):
            PK[i, 0:40] = r[i]
        s = {i: PK[i, 7:39] + PK[i, 8:40] for i in S_Y}
        d = {i: PK[i, 8:40] - PK[i, 7:39] for i in D_Y}
        high = ({i: pltpu.roll(v, 124, 1) for i, v in s.items()}, {i: pltpu.roll(v, 124, 1) for i, v in d.items()})
        for c, (u, w) in enumerate(x_parts((s, d), high)):
            WP[c] = u - w

    def from_low(w0, w1, packed, x):
        r0, r1 = pltpu.roll(w0, 1, 1), pltpu.roll(w1, 1, 1)
        edge = pltpu.roll(packed, 132 - 4 * x, 1) if x > 1 else packed
        return jnp.where(first_lane, edge, r0), jnp.where(first_lane, r0, r1)

    def forces(xs, finish):
        def body(g, carry):
            base = pl.multiple_of(8 + 8 * g, 8)
            own = pl.ds(pl.multiple_of(8 * g, 8), 8)
            packed = [WP[c, own, :] for c in range(3)]

            def sums(x):
                out = []
                for lt in range(2):
                    r1 = [R6[i, x, lt, pl.ds(base, 8), :] for i in range(6)]
                    r0 = [R6[i, x, lt, pl.ds(base - 1, 8), :] for i in range(6)]
                    out.append(({i: r0[i] + r1[i] for i in S_Y}, {i: r1[i] - r0[i] for i in D_Y}))
                return out

            low = sums(xs[0] - 1)
            for x in xs:
                high = sums(x)
                p0, p1 = x_parts(low[0], high[0]), x_parts(low[1], high[1])
                for c in range(3):
                    (u0, c0), (u1, c1) = p0[c], p1[c]
                    s0, s1 = from_low(u0 - c0, u1 - c1, packed[c], x)
                    finish(c, x, 0, base, own, u0 + c0 + s0)
                    finish(c, x, 1, base, own, u1 + c1 + s1)
                low = high
            return carry
        lax.fori_loop(0, 4, body, 0)

    TS[0, 0] = pack(U, 4, False, range(2, 6))
    TS[0, 1] = pack(U, 4, True, range(2, 6))
    for z in range(2):
        for x in range(4):
            LS[z, x] = line(TS[0, z], x + 2)

    t1 = tiles(0, TILES, t1s, t1r)
    l1 = lines(LINES, l1s, l1r)
    f1, x1 = along(sides(U, [d for d in SIDES if d[1]], 4, slice(2, 6), f1s, f1r))
    t2 = tiles(1, TILES, t2s, t2r)
    f2 = sides(FI, [(0, 1), (0, -1)], 3, slice(1, 8), f2s, f2r)
    t3 = tiles(2, LAST_TILES, t3s, t3r)
    f3 = sides(AD, [(0, -1)], 3, slice(2, 7), f3s, f3r)

    block = 1
    for i, n in zip(me, sizes):
        block = block * (1 + (i > 0).astype(jnp.int32) + (i < n - 1).astype(jnp.int32))
    pl.semaphore_wait(barrier, block - 1 + len(rings))

    send_across()
    start(l1)
    start(x1)
    start(t1)
    start(f1)
    start(thin)
    send_planes()
    relay_planes()

    def power(xs, total):
        def body(g, total):
            base = pl.multiple_of(8 * g, 8)
            rows = pl.ds(base, 8)
            own = pl.ds(pl.multiple_of(jnp.maximum(8 * g - 8, 0), 8), 8)
            inside = jnp.full((8, 128), g, jnp.int32) > 0
            for lt in range(2):
                low = y_sums(xs[0], lt, base)
                for x in xs:
                    high = y_sums(x + 1, lt, base)
                    e = strain6(gradients(low, high))
                    low = high
                    q, vm, w, r = load_terms(e, jnp.maximum(U[3, x, lt, rows, :], 0.0))
                    for i in range(6):
                        R6[i, x, lt, rows, :] = r[i]
                    if 2 <= x < 6:
                        v2 = vm * vm
                        total = total + jnp.where(inside, v2 * v2, 0.0)
                        tr = (LAM / 16.0) * (e[0] + e[1] + e[2])
                        for i in range(6):
                            S0[i, x - 2, lt, own, :] = tr + (MU / 8.0) * e[i] if i < 3 else (MU / 16.0) * e[i]
                        SE[x - 2, lt, own, :] = jnp.where(MT[x - 2, lt, own, :] == 1, (0.5 * BOOST) * (w * q), 0.0)
            return total
        return lax.fori_loop(0, 5, body, total)

    def fill_stiffness(xs):
        for x in xs:
            for lt in range(2):
                KF[x, lt, 0:40, :] = stiffness(U[3, x, lt, 0:40, :])

    def packed_load():
        d = pltpu.roll(PL[0, 0:40, :], 125, 1)
        kp = stiffness(d)
        packed_forces(load_terms(packed_strain(), jnp.maximum(d, 0.0))[3])
        PK[6, 0:40] = kp
        ky = PK[6, 7:39] + PK[6, 8:40]
        WP[3] = ky + pltpu.roll(ky, 124, 1)

    def diagonal(xs):
        def body(g, carry):
            base = pl.multiple_of(8 + 8 * g, 8)
            own = pl.ds(pl.multiple_of(8 * g, 8), 8)
            packed = WP[3, own, :]

            def sums(x):
                return [KF[x, lt, pl.ds(base, 8), :] + KF[x, lt, pl.ds(base - 1, 8), :] for lt in range(2)]

            low = sums(xs[0] - 1)
            for x in xs:
                high = sums(x)
                k0, k1 = low[0] + high[0], low[1] + high[1]
                s0, s1 = from_low(k0, k1, packed, x)
                for lt, k in ((0, k0 + s0), (1, k1 + s1)):
                    fixed = U[4, x, lt, pl.ds(base, 8), :]
                    FD[x, lt, own, :] = (1.0 - fixed) / (DIAG * k + fixed)
                low = high
            return carry
        lax.fori_loop(0, 4, body, 0)

    def first_out(c, x, lt, base, own, value):
        FI[c, x, lt, pl.ds(base, 8), :] = value * FD[x, lt, own, :]

    def ring(stage):
        buf = SUM if stage == 0 else SUM2
        return [pltpu.make_async_remote_copy(
            src_ref=buf.at[place[stage]], dst_ref=buf.at[place[stage]],
            send_sem=ass.at[i], recv_sem=asr.at[i], device_id=peer, device_id_type=MESH)
            for i, (a, peer) in enumerate(rings) if a == stage]

    def send_sum(stage, value):
        (SUM if stage == 0 else SUM2)[place[stage]] = value
        for c in ring(stage):
            c.start()

    def take_sum(stage):
        for c in ring(stage):
            c.wait_recv()
        buf, n = (SUM, nz) if stage == 0 else (SUM2, nx * ny)
        value = buf[0]
        for i in range(1, n):
            value = value + buf[i]
        return value

    arrive(t1)
    arrive(f1)
    for plane in range(3):
        merge(0, plane, False)
    packed_load()
    sweep_z(U, range(2, 6))
    total = power((2, 3, 4), jnp.zeros((8, 128), F32))
    fill_stiffness(range(2, 6))
    diagonal((3, 4, 5))
    forces((3, 4), first_out)

    arrive(l1)
    arrive(x1)
    for plane in range(3):
        merge(0, plane, True)
    packed_load()
    arrive_planes()
    sweep_z(U, (0, 1, 6, 7, 8))
    fill_stiffness((0, 1, 6, 7))
    diagonal((1, 2))
    diagonal((6, 7))
    total = power((5, 6, 7), total)
    send_sum(0, jnp.sum(total, axis=0, keepdims=True))
    power((0, 1), total)
    forces((1, 2), first_out)
    forces((5, 6, 7), first_out)
    start(f2)
    TS[1, 0] = pack(FI, 3, False, range(1, 8))
    TS[1, 1] = pack(FI, 3, True, range(1, 8))
    start(t2)
    send_sum(1, take_sum(0))

    def stiff(xs):
        def body(g, carry):
            base = pl.multiple_of(8 * g, 8)
            rows = pl.ds(base, 8)
            for lt in range(2):
                low = y_sums(xs[0], lt, base)
                for x in xs:
                    high = y_sums(x + 1, lt, base)
                    r = stiff_terms(strain6(gradients(low, high)), KF[x, lt, rows, :])
                    low = high
                    for i in range(6):
                        R6[i, x, lt, rows, :] = r[i]
            return carry
        lax.fori_loop(0, 5, body, 0)

    def packed_stiff():
        packed_forces(stiff_terms(packed_strain(), kp_ref[...]))

    def adjoint_out(c, x, lt, base, own, value):
        new = (1.0 + RELAX) * FI[c, x, lt, pl.ds(base, 8), :] - RELAX * FD[x, lt, own, :] * value
        AD[c, x, lt, pl.ds(base, 8), :] = new
        if x < 6:
            adj_out[c, x - 2, lt, own, :] = new

    kp_ref = PK.at[6, 0:40]
    arrive(t2)
    arrive(f2)
    for plane in range(3):
        merge(1, plane, False)
    packed_stiff()
    sweep_z(FI, range(1, 8))
    stiff(range(1, 7))
    forces(range(2, 7), adjoint_out)
    start(f3)
    TS[2, 0] = pack(AD, 3, False, range(2, 7))
    start(t3)

    def last(xs):
        def body(g, carry):
            base = pl.multiple_of(8 + 8 * g, 8)
            rows = pl.ds(base, 8)
            own = pl.ds(pl.multiple_of(8 * g, 8), 8)
            for lt in range(2):
                low = y_sums(xs[0] + 2, lt, base)
                for x in xs:
                    high = y_sums(x + 3, lt, base)
                    e = strain6(gradients(low, high))
                    low = high
                    dot = e[0] * S0[0, x, lt, own, :]
                    for i in range(1, 6):
                        dot = dot + e[i] * S0[i, x, lt, own, :]
                    d = U[3, x + 2, lt, rows, :]
                    slope = jnp.where(MT[x, lt, own, :] == 1, 3.0 * (d * d), 0.0)
                    sens_out[x, lt, own, :] = SE[x, lt, own, :] - slope * dot
            return carry
        lax.fori_loop(0, 4, body, 0)

    arrive(t3)
    arrive(f3)
    merge(2, 2, False)
    sweep_z(AD, range(2, 7))
    last((0, 1, 2, 3))
    sum_out[...] = take_sum(1)
    left_planes()
    for copies in (t1, l1, f1, x1, t2, f2, t3, f3):
        left(copies)
    for stage in range(2):
        for c in ring(stage):
            c.wait_send()


def finish_kernel(count, adj, sens, total, adj_out, sens_out):
    mean = jnp.full((8, 128), jnp.sum(total[...]) * (1.0 / count) + SHIFT, F32)
    scale = (jnp.sqrt(jnp.sqrt(jnp.sqrt(mean))) / mean * (1.0 / BOOST))[0:1]
    for x in range(4):
        for lt in range(2):
            cols = slice(128 * lt, 128 * lt + 128)
            sens_out[x, :, cols] = sens[x, lt] * scale
            for c in range(3):
                adj_out[c, x, :, cols] = adj[c, x, lt] * scale


def solution(mesh):
    sizes = tuple(mesh.shape[a] for a in ("gx", "gy", "gz"))
    peers = sizes[2] - 1 + sizes[0] * sizes[1] - 1
    count = sizes[0] * sizes[1] * sizes[2] * 4 * 32 * 256

    def per_device(displacement, density, material, fixed_mask):
        dma = pltpu.SemaphoreType.DMA
        vmem = pl.BlockSpec(memory_space=pltpu.VMEM)
        both = lambda n: [dma((n,)), dma((n,))]
        adj, sens, total = pl.pallas_call(
            functools.partial(kernel, sizes),
            out_shape=(pltpu.VMEM((3, 4, 2, 32, 128), F32), pltpu.VMEM((4, 2, 32, 128), F32), pltpu.VMEM((1, 128), F32)),
            in_specs=[pl.BlockSpec(memory_space=pl.ANY)] * 4,
            out_specs=[vmem] * 3,
            scratch_shapes=[
                pltpu.VMEM((5, 9, 2, ROWS, 128), F32),
                pltpu.VMEM((3, 9, 2, ROWS, 128), F32),
                pltpu.VMEM((3, 9, 2, ROWS, 128), F32),
                pltpu.VMEM((4, 2, 32, 128), F32),
                pltpu.VMEM((4, 2, 32, 128), jnp.int32),
                pltpu.VMEM((4, 2, 32, 128), jnp.int32),
                pltpu.VMEM((3, 9, 2, ROWS, 128), F32),
                pltpu.VMEM((3, 9, 2, ROWS, 128), F32),
                pltpu.VMEM((6, 8, 2, ROWS, 128), F32),
                pltpu.VMEM((8, 2, ROWS, 128), F32),
                pltpu.VMEM((6, 4, 2, 32, 128), F32),
                pltpu.VMEM((4, 2, 32, 128), F32),
                pltpu.VMEM((8, 2, 32, 128), F32),
                pltpu.VMEM((3, 2, 8, 128), F32),
                pltpu.VMEM((2, 4, 1, 128), F32),
                pltpu.VMEM((3, 3, 3, 8, 128), F32),
                pltpu.VMEM((3, 2, 3, 3, 1, 128), F32),
                pltpu.VMEM((3, ROWS, 128), F32),
                pltpu.VMEM((7, ROWS, 128), F32),
                pltpu.VMEM((4, 32, 128), F32),
                pltpu.VMEM((sizes[2], 1, 128), F32),
                pltpu.VMEM((sizes[0] * sizes[1], 1, 128), F32),
                pltpu.VMEM((3, 3, 2, 32, 128), F32),
                dma((8,)),
                *both(4), *both(12), *both(6), *both(8), *both(18),
                *both(2), *both(8), *both(1), *both(2),
                *both(peers),
            ],
            compiler_params=pltpu.CompilerParams(collective_id=0, has_side_effects=True),
        )(displacement, density, material, fixed_mask)
        return pl.pallas_call(
            functools.partial(finish_kernel, count),
            out_shape=(jax.ShapeDtypeStruct((3, 4, 32, 256), F32), jax.ShapeDtypeStruct((4, 32, 256), F32)),
            in_specs=[vmem] * 3,
            out_specs=[vmem] * 2,
        )(*(pltpu.with_memory_space_constraint(v, pltpu.VMEM) for v in (adj, sens, total)))

    placed = (P(None, "gx", "gy", "gz"), P("gx", "gy", "gz"), P("gx", "gy", "gz"), P("gx", "gy", "gz"))
    return jax.shard_map(per_device, mesh=mesh, in_specs=placed, out_specs=(placed[0], placed[1]), check_vma=False)
```

```python
import functools
import itertools

import jax
import jax.numpy as jnp
from jax import lax
from jax.experimental import pallas as pl
from jax.experimental.pallas import tpu as pltpu
from jax.sharding import PartitionSpec as P

LAM = 0.577
MU = 0.385
DIAG = (0.577 + 4.0 * 0.385) / 16.0
RELAX = 0.6
SHIFT = 1e-06
BOOST = 2.0**18
MESH = pl.DeviceIdType.MESH
ROUTE = (0, 1, 2)
ORDER = (0, 1, 2)
F32 = jnp.float32
ROWS = 48
NEAR = [d for d in itertools.product((-1, 0, 1), repeat=3) if d != (0, 0, 0)]
SIDES = [d for d in itertools.product((-1, 0, 1), repeat=2) if d != (0, 0)]
TILES = [d for d in NEAR if d[0] == 0]
LINES = [d for d in NEAR if d[0] != 0]
LAST_TILES = [(0, 0, -1), (0, -1, -1)]
OUTSIDE = (0.0, 0.0, 0.0, -1.0, 1.0)


def span(step):
    return {1: (slice(4, 6), slice(0, 2)), -1: (slice(2, 5), slice(6, 9)), 0: (slice(2, 6), slice(2, 6))}[step]


def rows_of(step):
    return {1: (slice(39, 40), slice(7, 8)), -1: (slice(8, 9), slice(40, 41)), 0: (slice(8, 40), slice(8, 40))}[step]


def kernel(sizes, disp, dens, mat, fix, adj_out, sens_out, sum_out, *scratch):
    (U, FI, AD, DN, MT, FX, PS, QS, R6, KF, S0, SE, FD, TS, LS, TR, LR, PL, PK, WP, SUM, SUM2, ST, in_sem,
     xs_, xr_, hs_, hr_, f1s, f1r, t1s, t1r, l1s, l1r, f2s, f2r, t2s, t2r, f3s, f3r, t3s, t3r, ass, asr) = scratch
    nx, ny, nz = sizes
    me = (lax.axis_index("gx"), lax.axis_index("gy"), lax.axis_index("gz"))
    lane = lax.broadcasted_iota(jnp.int32, (8, 128), 1)
    sub = lax.broadcasted_iota(jnp.int32, (8, 128), 0)
    first_lane = lane == 0
    last_lane = lane == 127

    def exists(step):
        ok = None
        for i, s, n in zip(me, step, sizes):
            if s:
                one = i < n - 1 if s > 0 else i > 0
                ok = one if ok is None else jnp.logical_and(ok, one)
        return ok

    def at(step):
        return tuple(i + s for i, s in zip(me, step))

    def back(step):
        return tuple(-s for s in step)

    barrier = pltpu.get_barrier_semaphore()

    def greet(device):
        pl.semaphore_signal(barrier, inc=1, device_id=device, device_id_type=MESH)

    place = (me[2], me[0] * ny + me[1])
    rings = []
    for k in range(1, nz):
        rings.append((0, (me[0], me[1], lax.rem(me[2] + k, nz))))
    for k in range(1, nx * ny):
        other = lax.rem(place[1] + k, nx * ny)
        rings.append((1, (other // ny, lax.rem(other, ny), me[2])))
    for _, peer in rings:
        greet(peer)
    for step in NEAR:
        pl.when(exists(step))(functools.partial(greet, at(step)))

    loads = []
    for lt in range(2):
        cols = pl.ds(lt * 128, 128)
        loads.append(pltpu.make_async_copy(disp.at[:, :, :, cols], U.at[0:3, 2:6, lt, 8:40, :], in_sem.at[4 * lt]))
        loads.append(pltpu.make_async_copy(dens.at[:, :, cols], DN.at[:, lt], in_sem.at[4 * lt + 1]))
        loads.append(pltpu.make_async_copy(mat.at[:, :, cols], MT.at[:, lt], in_sem.at[4 * lt + 2]))
        loads.append(pltpu.make_async_copy(fix.at[:, :, cols], FX.at[:, lt], in_sem.at[4 * lt + 3]))
    for c in loads:
        c.start()

    def plane_of(step):
        return 1 - step[2]

    def clear(k, ref, comps):
        for step, row in (((0, -1, 0), 7), ((0, 1, 0), 40)):
            def fill(row=row):
                for c in range(comps):
                    for x in range(9):
                        for lt in range(2):
                            ref[c, x, lt, row : row + 1, :] = jnp.full((1, 128), OUTSIDE[c], F32)
            pl.when(jnp.logical_not(exists(step)))(fill)
        for step in TILES:
            def fill(step=step):
                TR[k, plane_of(step), step[1] + 1] = outside
            pl.when(jnp.logical_not(exists(back(step))))(fill)

    outside = jnp.where(lane % 4 == 3, -1.0, 0.0)
    for step, planes in (((-1, 0, 0), (0, 1)), ((1, 0, 0), (6, 7, 8))):
        def fill(planes=planes):
            for c in range(5):
                for x in planes:
                    for lt in range(2):
                        U[c, x, lt, 7:41, :] = jnp.full((34, 128), OUTSIDE[c], F32)
        pl.when(jnp.logical_not(exists(step)))(fill)
    for step in LINES:
        def fill(step=step):
            for i in range(3):
                LR[plane_of(step), (1 - step[0]) // 2, step[1] + 1, i] = outside[0:1]
        pl.when(jnp.logical_not(exists(back(step))))(fill)
    clear(0, U, 4)
    clear(1, FI, 3)
    clear(2, AD, 3)
    for c in loads:
        c.wait()

    for x in range(4):
        for lt in range(2):
            m = MT[x, lt]
            U[3, x + 2, lt, 8:40, :] = jnp.where(m == 1, DN[x, lt], jnp.where(m == 2, 1.0, 0.0))
            U[4, x + 2, lt, 8:40, :] = FX[x, lt].astype(F32)

    def pack(ref, comps, high, xs):
        lt, source = (1, 127) if high else (0, 0)
        parts = []
        for g in range(4):
            part = jnp.zeros((8, 128), F32)
            for c in range(comps):
                for x in xs:
                    to = 32 * g + 4 * x + c
                    v = ref[c, x, lt, 8 + 8 * g : 16 + 8 * g, :]
                    part = jnp.where(lane == to, pltpu.roll(v, (to - source) % 128, 1), part)
            parts.append(part)
        return (parts[0] + parts[1]) + (parts[2] + parts[3])

    def line(tile, x):
        out = jnp.zeros((8, 128), F32)
        mine = (lane % 32) // 4 == 7 - sub
        for i in range(8):
            out = jnp.where(jnp.logical_and(mine, sub == i), pltpu.roll(tile, (28 - 4 * i - 4 * x) % 128, 1), out)
        return jnp.sum(out, axis=0, keepdims=True)

    def spread(row, x):
        moved = pltpu.roll(jnp.broadcast_to(row, (8, 128)), 0, 1, stride=4, stride_axis=0)
        return pltpu.roll(moved, (100 + 4 * x) % 128, 1)

    def remote(src, dst, send, recv, step):
        return (step, pltpu.make_async_remote_copy(
            src_ref=src, dst_ref=dst, send_sem=send, recv_sem=recv, device_id=at(step), device_id_type=MESH))

    def sides(ref, steps, comps, planes, send, recv):
        out = []
        for i, (dx, dy) in enumerate(steps):
            (sx, tx), (sr, tr) = span(dx) if dx else (planes, planes), rows_of(dy)
            out.append(remote(ref.at[0:comps, sx, :, sr, :], ref.at[0:comps, tx, :, tr, :], send.at[i], recv.at[i], (dx, dy, 0)))
        return out

    def tiles(k, steps, send, recv):
        return [remote(TS.at[k, 1 if step[2] > 0 else 0], TR.at[k, plane_of(step), step[1] + 1], send.at[i], recv.at[i], step)
                for i, step in enumerate(steps)]

    def lines(steps, send, recv):
        out = []
        for i, step in enumerate(steps):
            planes, count, side = (slice(2, 4), 2, 0) if step[0] > 0 else (slice(0, 3), 3, 1)
            out.append(remote(LS.at[1 if step[2] > 0 else 0, planes], LR.at[plane_of(step), side, step[1] + 1, 0:count],
                              send.at[i], recv.at[i], step))
        return out

    middle = nx // 2
    own = slice(8, 40)

    def plane_copy(comps, src, dst, i, step):
        return remote(U.at[comps, src, :, own, :], U.at[comps, dst, :, own, :], xs_.at[i], xr_.at[i], step)

    wide = [plane_copy(slice(0, 3), slice(4, 6), slice(0, 2), 0, (1, 0, 0)), plane_copy(slice(0, 3), slice(2, 5), slice(6, 9), 1, (-1, 0, 0))]
    thin = [plane_copy(slice(3, 5), slice(4, 6), slice(0, 2), 2, (1, 0, 0)), plane_copy(slice(3, 5), slice(2, 4), slice(6, 8), 3, (-1, 0, 0))]
    low_side, high_side = me[0] == middle - 1, me[0] == middle

    def plain(step):
        return jnp.logical_and(exists(step), jnp.logical_not(low_side if step[0] > 0 else high_side))

    def hop(c, up, leg):
        count = 2 if up else 3
        src = U.at[c, slice(4, 6) if up else slice(2, 5), :, own, :]
        dst = U.at[c, slice(0, 2) if up else slice(6, 9), :, own, :]
        stage = ST.at[c, 0:count]
        if leg == 0:
            pair, to = (src, stage), relay_of(c, up)
        else:
            pair, to = (src if ROUTE[c] is None else stage, dst), (middle if up else middle - 1)
        i = (2 * c + (0 if up else 1)) * 2 + leg
        return pltpu.make_async_remote_copy(src_ref=pair[0], dst_ref=pair[1], send_sem=hs_.at[i], recv_sem=hr_.at[i],
                                            device_id=(to, me[1], me[2]), device_id_type=MESH)

    def relay_of(c, up):
        return ROUTE[c] if up else nx - 1 - ROUTE[c]

    crossings = [(c, up, low_side if up else high_side, high_side if up else low_side) for c in ORDER for up in (True, False)]

    def send_across():
        for c, up, here, _ in crossings:
            pl.when(here)(hop(c, up, 1 if ROUTE[c] is None else 0).start)

    def send_planes():
        for step, c in wide:
            pl.when(plain(step))(c.start)

    def relay_planes():
        for c, up, _, _ in crossings:
            if ROUTE[c] is not None:
                def forward(c=c, up=up):
                    hop(c, up, 0).wait_recv()
                    hop(c, up, 1).start()
                pl.when(me[0] == relay_of(c, up))(forward)

    def arrive_planes():
        for step, c in wide:
            pl.when(plain(back(step)))(c.wait_recv)
        for c, up, _, there in crossings:
            pl.when(there)(hop(c, up, 1).wait_recv)

    def left_planes():
        left(thin)
        for step, c in wide:
            pl.when(plain(step))(c.wait_send)
        for c, up, here, _ in crossings:
            if ROUTE[c] is None:
                pl.when(here)(hop(c, up, 1).wait_send)
            else:
                pl.when(here)(hop(c, up, 0).wait_send)
                pl.when(me[0] == relay_of(c, up))(hop(c, up, 1).wait_send)

    def along(copies):
        return [c for c in copies if c[0][0] == 0], [c for c in copies if c[0][0] != 0]

    def start(copies):
        for step, c in copies:
            pl.when(exists(step))(c.start)

    def arrive(copies):
        for step, c in copies:
            pl.when(exists(back(step)))(c.wait_recv)

    def left(copies):
        for step, c in copies:
            pl.when(exists(step))(c.wait_send)

    def merge(k, plane, with_x):
        for dy in (-1, 0, 1):
            full = TS[k, 0] if plane == 1 and dy == 0 else TR[k, plane, dy + 1]
            if with_x:
                for side, i, x in ((0, 0, 0), (0, 1, 1), (1, 0, 6), (1, 1, 7)):
                    here = jnp.logical_and(lane % 32 >= 4 * x, lane % 32 < 4 * x + 4)
                    full = jnp.where(here, spread(LR[plane, side, dy + 1, i], x), full)
                far = spread(LR[plane, 1, dy + 1, 2], 0)

            def unfold(shift):
                part = pltpu.roll(full, shift, 1) if shift else full
                if with_x:
                    part = jnp.where(jnp.logical_and(lane >= 32, lane < 36), pltpu.roll(far, (shift + 32) % 128, 1), part)
                return part

            if dy == 0:
                for g in range(4):
                    PL[plane, 8 + 8 * g : 16 + 8 * g, :] = unfold((128 - 32 * g) % 128)
            elif dy == 1:
                PL[plane, 0:8, :] = unfold(32)
            else:
                PL[plane, 40:48, :] = unfold(0)

    def sweep_z(ref, xs, lts=(0, 1), begin=7, count=5, stride=8):
        def body(g, carry):
            rows = pl.ds(begin + stride * g, 8)
            edge = PL[2, rows, :] if 1 in lts else None
            for c in range(3):
                for x in xs:
                    t1 = ref[c, x, 1, rows, :]
                    r1 = pltpu.roll(t1, 127, 1)
                    if 0 in lts:
                        t0 = ref[c, x, 0, rows, :]
                        s0 = jnp.where(last_lane, r1, pltpu.roll(t0, 127, 1))
                        PS[c, x, 0, rows, :] = s0 + t0
                        QS[c, x, 0, rows, :] = s0 - t0
                    if 1 in lts:
                        s1 = jnp.where(last_lane, pltpu.roll(edge, 127 - 4 * x - c, 1), r1)
                        PS[c, x, 1, rows, :] = s1 + t1
                        QS[c, x, 1, rows, :] = s1 - t1
            return carry
        lax.fori_loop(0, count, body, 0)

    def gradients(low, high):
        return [[high[c][0] - low[c][0] for c in range(3)], [high[c][1] + low[c][1] for c in range(3)],
                [high[c][2] + low[c][2] for c in range(3)]]

    def strain6(g):
        gx, gy, gz = g
        return gx[0], gy[1], gz[2], gy[0] + gx[1], gz[1] + gy[2], gx[2] + gz[0]

    def y_sums(x, lt, base):
        out = []
        for c in range(3):
            p0, p1 = PS[c, x, lt, pl.ds(base, 8), :], PS[c, x, lt, pl.ds(base + 1, 8), :]
            q0, q1 = QS[c, x, lt, pl.ds(base, 8), :], QS[c, x, lt, pl.ds(base + 1, 8), :]
            out.append((p0 + p1, p1 - p0, q0 + q1))
        return out

    def packed_strain():
        lo, hi = PL[0], PL[1]
        PK[0] = lo + hi
        PK[1] = hi - lo
        p0, p1, q0, q1 = PK[0, 0:40], PK[0, 1:41], PK[1, 0:40], PK[1, 1:41]
        a, b, c = p0 + p1, p1 - p0, q0 + q1
        g = [pltpu.roll(a, 124, 1) - a, pltpu.roll(b, 124, 1) + b, pltpu.roll(c, 124, 1) + c]
        return strain6([[t] + [pltpu.roll(t, 128 - i, 1) for i in (1, 2)] for t in g])

    def stiffness(d):
        return jnp.where(d < 0.0, 0.0, 0.001 + d * d * d)

    def load_terms(e, d):
        a, b, c = e[0] - e[1], e[1] - e[2], e[2] - e[0]
        q = (MU * MU / 16.0) * (2.0 * (a * a + b * b + c * c) + 3.0 * (e[3] * e[3] + e[4] * e[4] + e[5] * e[5]))
        vm = d * q
        w = vm * vm * vm
        t = (-MU * MU / 8.0 * BOOST) * (w * d)
        ts = 1.5 * t
        return q, vm, w, (t * (a - c), t * (b - a), t * (c - b), ts * e[3], ts * e[4], ts * e[5])

    def stiff_terms(e, kf):
        k = kf * (-2.0 * MU / 16.0)
        tr = (kf * (-LAM / 16.0)) * (e[0] + e[1] + e[2])
        ks = kf * (-MU / 16.0)
        return tr + k * e[0], tr + k * e[1], tr + k * e[2], ks * e[3], ks * e[4], ks * e[5]

    S_Y, D_Y = (0, 3, 5, 4, 2), (3, 1, 4)

    def x_parts(low, high):
        (sl, dl), (sh, dh) = low, high
        return [((sh[i] - sl[i]) + (dh[j] + dl[j]), sh[k] + sl[k]) for i, j, k in ((0, 3, 5), (3, 1, 4), (5, 4, 2))]

    def packed_forces(r):
        for i in range(6):
            PK[i, 0:40] = r[i]
        s = {i: PK[i, 7:39] + PK[i, 8:40] for i in S_Y}
        d = {i: PK[i, 8:40] - PK[i, 7:39] for i in D_Y}
        high = ({i: pltpu.roll(v, 124, 1) for i, v in s.items()}, {i: pltpu.roll(v, 124, 1) for i, v in d.items()})
        for c, (u, w) in enumerate(x_parts((s, d), high)):
            WP[c] = u - w

    def from_low(w0, w1, packed, x):
        r0, r1 = pltpu.roll(w0, 1, 1), pltpu.roll(w1, 1, 1)
        edge = pltpu.roll(packed, 132 - 4 * x, 1) if x > 1 else packed
        return jnp.where(first_lane, edge, r0), jnp.where(first_lane, r0, r1)

    def forces(xs, finish):
        def body(g, carry):
            base = pl.multiple_of(8 + 8 * g, 8)
            own = pl.ds(pl.multiple_of(8 * g, 8), 8)
            packed = [WP[c, own, :] for c in range(3)]

            def sums(x):
                out = []
                for lt in range(2):
                    r1 = [R6[i, x, lt, pl.ds(base, 8), :] for i in range(6)]
                    r0 = [R6[i, x, lt, pl.ds(base - 1, 8), :] for i in range(6)]
                    out.append(({i: r0[i] + r1[i] for i in S_Y}, {i: r1[i] - r0[i] for i in D_Y}))
                return out

            low = sums(xs[0] - 1)
            for x in xs:
                high = sums(x)
                p0, p1 = x_parts(low[0], high[0]), x_parts(low[1], high[1])
                for c in range(3):
                    (u0, c0), (u1, c1) = p0[c], p1[c]
                    s0, s1 = from_low(u0 - c0, u1 - c1, packed[c], x)
                    finish(c, x, 0, base, own, u0 + c0 + s0)
                    finish(c, x, 1, base, own, u1 + c1 + s1)
                low = high
            return carry
        lax.fori_loop(0, 4, body, 0)

    TS[0, 0] = pack(U, 4, False, range(2, 6))
    TS[0, 1] = pack(U, 4, True, range(2, 6))
    for z in range(2):
        for x in range(4):
            LS[z, x] = line(TS[0, z], x + 2)

    t1 = tiles(0, TILES, t1s, t1r)
    l1 = lines(LINES, l1s, l1r)
    f1, x1 = along(sides(U, [d for d in SIDES if d[1]], 4, slice(2, 6), f1s, f1r))
    t2 = tiles(1, TILES, t2s, t2r)
    f2 = sides(FI, [(0, 1), (0, -1)], 3, slice(1, 8), f2s, f2r)
    t3 = tiles(2, LAST_TILES, t3s, t3r)
    f3 = sides(AD, [(0, -1)], 3, slice(2, 7), f3s, f3r)

    block = 1
    for i, n in zip(me, sizes):
        block = block * (1 + (i > 0).astype(jnp.int32) + (i < n - 1).astype(jnp.int32))
    pl.semaphore_wait(barrier, block - 1 + len(rings))

    send_across()
    start(l1)
    start(x1)
    start(t1)
    start(f1)
    start(thin)
    send_planes()
    relay_planes()

    def power(xs, total):
        def body(g, total):
            base = pl.multiple_of(8 * g, 8)
            rows = pl.ds(base, 8)
            own = pl.ds(pl.multiple_of(jnp.maximum(8 * g - 8, 0), 8), 8)
            inside = jnp.full((8, 128), g, jnp.int32) > 0
            for lt in range(2):
                low = y_sums(xs[0], lt, base)
                for x in xs:
                    high = y_sums(x + 1, lt, base)
                    e = strain6(gradients(low, high))
                    low = high
                    q, vm, w, r = load_terms(e, jnp.maximum(U[3, x, lt, rows, :], 0.0))
                    for i in range(6):
                        R6[i, x, lt, rows, :] = r[i]
                    if 2 <= x < 6:
                        v2 = vm * vm
                        total = total + jnp.where(inside, v2 * v2, 0.0)
                        tr = (LAM / 16.0) * (e[0] + e[1] + e[2])
                        for i in range(6):
                            S0[i, x - 2, lt, own, :] = tr + (MU / 8.0) * e[i] if i < 3 else (MU / 16.0) * e[i]
                        SE[x - 2, lt, own, :] = jnp.where(MT[x - 2, lt, own, :] == 1, (0.5 * BOOST) * (w * q), 0.0)
            return total
        return lax.fori_loop(0, 5, body, total)

    def fill_stiffness(xs):
        for x in xs:
            for lt in range(2):
                KF[x, lt, 0:40, :] = stiffness(U[3, x, lt, 0:40, :])

    def packed_load():
        d = pltpu.roll(PL[0, 0:40, :], 125, 1)
        kp = stiffness(d)
        packed_forces(load_terms(packed_strain(), jnp.maximum(d, 0.0))[3])
        PK[6, 0:40] = kp
        ky = PK[6, 7:39] + PK[6, 8:40]
        WP[3] = ky + pltpu.roll(ky, 124, 1)

    def diagonal(xs):
        def body(g, carry):
            base = pl.multiple_of(8 + 8 * g, 8)
            own = pl.ds(pl.multiple_of(8 * g, 8), 8)
            packed = WP[3, own, :]

            def sums(x):
                return [KF[x, lt, pl.ds(base, 8), :] + KF[x, lt, pl.ds(base - 1, 8), :] for lt in range(2)]

            low = sums(xs[0] - 1)
            for x in xs:
                high = sums(x)
                k0, k1 = low[0] + high[0], low[1] + high[1]
                s0, s1 = from_low(k0, k1, packed, x)
                for lt, k in ((0, k0 + s0), (1, k1 + s1)):
                    fixed = U[4, x, lt, pl.ds(base, 8), :]
                    FD[x, lt, own, :] = (1.0 - fixed) / (DIAG * k + fixed)
                low = high
            return carry
        lax.fori_loop(0, 4, body, 0)

    def first_out(c, x, lt, base, own, value):
        FI[c, x, lt, pl.ds(base, 8), :] = value * FD[x, lt, own, :]

    def ring(stage):
        buf = SUM if stage == 0 else SUM2
        return [pltpu.make_async_remote_copy(
            src_ref=buf.at[place[stage]], dst_ref=buf.at[place[stage]],
            send_sem=ass.at[i], recv_sem=asr.at[i], device_id=peer, device_id_type=MESH)
            for i, (a, peer) in enumerate(rings) if a == stage]

    def send_sum(stage, value):
        (SUM if stage == 0 else SUM2)[place[stage]] = value
        for c in ring(stage):
            c.start()

    def take_sum(stage):
        for c in ring(stage):
            c.wait_recv()
        buf, n = (SUM, nz) if stage == 0 else (SUM2, nx * ny)
        value = buf[0]
        for i in range(1, n):
            value = value + buf[i]
        return value

    arrive(t1)
    arrive(f1)
    for plane in range(3):
        merge(0, plane, False)
    packed_load()
    sweep_z(U, range(2, 6))
    total = power((2, 3, 4), jnp.zeros((8, 128), F32))
    fill_stiffness(range(2, 6))
    diagonal((3, 4, 5))
    forces((3, 4), first_out)

    arrive(l1)
    arrive(x1)
    for plane in range(3):
        merge(0, plane, True)
    packed_load()
    arrive(thin)
    fill_stiffness((0, 1, 6, 7))
    diagonal((1, 2))
    diagonal((6, 7))
    arrive_planes()
    sweep_z(U, (0, 1, 6, 7, 8))
    total = power((5, 6, 7), total)
    send_sum(0, jnp.sum(total, axis=0, keepdims=True))
    power((0, 1), total)
    forces((1, 2), first_out)
    forces((5, 6, 7), first_out)
    start(f2)
    TS[1, 0] = pack(FI, 3, False, range(1, 8))
    TS[1, 1] = pack(FI, 3, True, range(1, 8))
    start(t2)

    def stiff(xs, lts, begin, count, stride):
        def body(g, carry):
            base = pl.multiple_of(begin + stride * g, 8)
            rows = pl.ds(base, 8)
            for lt in lts:
                low = y_sums(xs[0], lt, base)
                for x in xs:
                    high = y_sums(x + 1, lt, base)
                    r = stiff_terms(strain6(gradients(low, high)), KF[x, lt, rows, :])
                    low = high
                    for i in range(6):
                        R6[i, x, lt, rows, :] = r[i]
            return carry
        lax.fori_loop(0, count, body, 0)

    def packed_stiff():
        packed_forces(stiff_terms(packed_strain(), kp_ref[...]))

    def adjoint_out(c, x, lt, base, own, value):
        new = (1.0 + RELAX) * FI[c, x, lt, pl.ds(base, 8), :] - RELAX * FD[x, lt, own, :] * value
        AD[c, x, lt, pl.ds(base, 8), :] = new
        if x < 6:
            adj_out[c, x - 2, lt, own, :] = new

    kp_ref = PK.at[6, 0:40]
    sweep_z(FI, range(1, 8), (0,), 8, 4)
    stiff(range(1, 7), (0,), 8, 3, 8)
    send_sum(1, take_sum(0))
    arrive(t2)
    arrive(f2)
    for plane in range(3):
        merge(1, plane, False)
    packed_stiff()
    sweep_z(FI, range(1, 8), (1,))
    sweep_z(FI, range(1, 8), (0,), 0, 2, 40)
    stiff(range(1, 7), (0,), 0, 2, 32)
    stiff(range(1, 7), (1,), 0, 5, 8)
    forces(range(2, 7), adjoint_out)
    start(f3)
    TS[2, 0] = pack(AD, 3, False, range(2, 7))
    start(t3)

    def last(xs, lts, begin, count):
        def body(g, carry):
            base = pl.multiple_of(begin + 8 * g, 8)
            rows = pl.ds(base, 8)
            own = pl.ds(pl.multiple_of(begin - 8 + 8 * g, 8), 8)
            for lt in lts:
                low = y_sums(xs[0] + 2, lt, base)
                for x in xs:
                    high = y_sums(x + 3, lt, base)
                    e = strain6(gradients(low, high))
                    low = high
                    dot = e[0] * S0[0, x, lt, own, :]
                    for i in range(1, 6):
                        dot = dot + e[i] * S0[i, x, lt, own, :]
                    d = U[3, x + 2, lt, rows, :]
                    slope = jnp.where(MT[x, lt, own, :] == 1, 3.0 * (d * d), 0.0)
                    sens_out[x, lt, own, :] = SE[x, lt, own, :] - slope * dot
            return carry
        lax.fori_loop(0, count, body, 0)

    sweep_z(AD, range(2, 7), (0,), 8, 4)
    last((0, 1, 2, 3), (0,), 8, 3)
    arrive(t3)
    arrive(f3)
    merge(2, 2, False)
    sweep_z(AD, range(2, 7), (1,))
    sweep_z(AD, range(2, 7), (0,), 40, 1)
    last((0, 1, 2, 3), (0,), 32, 1)
    last((0, 1, 2, 3), (1,), 8, 4)
    sum_out[...] = take_sum(1)
    left_planes()
    for copies in (t1, l1, f1, x1, t2, f2, t3, f3):
        left(copies)
    for stage in range(2):
        for c in ring(stage):
            c.wait_send()


def finish_kernel(count, adj, sens, total, adj_out, sens_out):
    mean = jnp.full((8, 128), jnp.sum(total[...]) * (1.0 / count) + SHIFT, F32)
    scale = (jnp.sqrt(jnp.sqrt(jnp.sqrt(mean))) / mean * (1.0 / BOOST))[0:1]
    for x in range(4):
        for lt in range(2):
            cols = slice(128 * lt, 128 * lt + 128)
            sens_out[x, :, cols] = sens[x, lt] * scale
            for c in range(3):
                adj_out[c, x, :, cols] = adj[c, x, lt] * scale


def solution(mesh):
    sizes = tuple(mesh.shape[a] for a in ("gx", "gy", "gz"))
    peers = sizes[2] - 1 + sizes[0] * sizes[1] - 1
    count = sizes[0] * sizes[1] * sizes[2] * 4 * 32 * 256

    def per_device(displacement, density, material, fixed_mask):
        dma = pltpu.SemaphoreType.DMA
        vmem = pl.BlockSpec(memory_space=pltpu.VMEM)
        both = lambda n: [dma((n,)), dma((n,))]
        adj, sens, total = pl.pallas_call(
            functools.partial(kernel, sizes),
            out_shape=(pltpu.VMEM((3, 4, 2, 32, 128), F32), pltpu.VMEM((4, 2, 32, 128), F32), pltpu.VMEM((1, 128), F32)),
            in_specs=[pl.BlockSpec(memory_space=pl.ANY)] * 4,
            out_specs=[vmem] * 3,
            scratch_shapes=[
                pltpu.VMEM((5, 9, 2, ROWS, 128), F32),
                pltpu.VMEM((3, 9, 2, ROWS, 128), F32),
                pltpu.VMEM((3, 9, 2, ROWS, 128), F32),
                pltpu.VMEM((4, 2, 32, 128), F32),
                pltpu.VMEM((4, 2, 32, 128), jnp.int32),
                pltpu.VMEM((4, 2, 32, 128), jnp.int32),
                pltpu.VMEM((3, 9, 2, ROWS, 128), F32),
                pltpu.VMEM((3, 9, 2, ROWS, 128), F32),
                pltpu.VMEM((6, 8, 2, ROWS, 128), F32),
                pltpu.VMEM((8, 2, ROWS, 128), F32),
                pltpu.VMEM((6, 4, 2, 32, 128), F32),
                pltpu.VMEM((4, 2, 32, 128), F32),
                pltpu.VMEM((8, 2, 32, 128), F32),
                pltpu.VMEM((3, 2, 8, 128), F32),
                pltpu.VMEM((2, 4, 1, 128), F32),
                pltpu.VMEM((3, 3, 3, 8, 128), F32),
                pltpu.VMEM((3, 2, 3, 3, 1, 128), F32),
                pltpu.VMEM((3, ROWS, 128), F32),
                pltpu.VMEM((7, ROWS, 128), F32),
                pltpu.VMEM((4, 32, 128), F32),
                pltpu.VMEM((sizes[2], 1, 128), F32),
                pltpu.VMEM((sizes[0] * sizes[1], 1, 128), F32),
                pltpu.VMEM((3, 3, 2, 32, 128), F32),
                dma((8,)),
                *both(4), *both(12), *both(6), *both(8), *both(18),
                *both(2), *both(8), *both(1), *both(2),
                *both(peers),
            ],
            compiler_params=pltpu.CompilerParams(collective_id=0, has_side_effects=True),
        )(displacement, density, material, fixed_mask)
        return pl.pallas_call(
            functools.partial(finish_kernel, count),
            out_shape=(jax.ShapeDtypeStruct((3, 4, 32, 256), F32), jax.ShapeDtypeStruct((4, 32, 256), F32)),
            in_specs=[vmem] * 3,
            out_specs=[vmem] * 2,
        )(*(pltpu.with_memory_space_constraint(v, pltpu.VMEM) for v in (adj, sens, total)))

    placed = (P(None, "gx", "gy", "gz"), P("gx", "gy", "gz"), P("gx", "gy", "gz"), P("gx", "gy", "gz"))
    return jax.shard_map(per_device, mesh=mesh, in_specs=placed, out_specs=(placed[0], placed[1]), check_vma=False)
```

```python
import functools
import itertools

import jax
import jax.numpy as jnp
from jax import lax
from jax.experimental import pallas as pl
from jax.experimental.pallas import tpu as pltpu
from jax.sharding import PartitionSpec as P

LAM = 0.577
MU = 0.385
DIAG = (0.577 + 4.0 * 0.385) / 16.0
RELAX = 0.6
SHIFT = 1e-06
BOOST = 2.0**18
MESH = pl.DeviceIdType.MESH
ROUTE = (0, 1, 2)
ORDER = (0, 1, 2)
F32 = jnp.float32
ROWS = 48
NEAR = [d for d in itertools.product((-1, 0, 1), repeat=3) if d != (0, 0, 0)]
SIDES = [d for d in itertools.product((-1, 0, 1), repeat=2) if d != (0, 0)]
TILES = [d for d in NEAR if d[0] == 0]
LINES = [d for d in NEAR if d[0] != 0]
LAST_TILES = [(0, 0, -1), (0, -1, -1)]
OUTSIDE = (0.0, 0.0, 0.0, -1.0, 1.0)


def span(step):
    return {1: (slice(4, 6), slice(0, 2)), -1: (slice(2, 5), slice(6, 9)), 0: (slice(2, 6), slice(2, 6))}[step]


def rows_of(step):
    return {1: (slice(39, 40), slice(7, 8)), -1: (slice(8, 9), slice(40, 41)), 0: (slice(8, 40), slice(8, 40))}[step]


def kernel(sizes, disp, dens, mat, fix, adj_out, sens_out, sum_out, *scratch):
    (U, FI, AD, DN, MT, FX, PS, QS, R6, KF, S0, SE, FD, TS, LS, TR, LR, PL, PK, WP, SUM, SUM2, ST, in_sem,
     xs_, xr_, hs_, hr_, f1s, f1r, t1s, t1r, l1s, l1r, f2s, f2r, t2s, t2r, f3s, f3r, t3s, t3r, ass, asr) = scratch
    nx, ny, nz = sizes
    me = (lax.axis_index("gx"), lax.axis_index("gy"), lax.axis_index("gz"))
    lane = lax.broadcasted_iota(jnp.int32, (8, 128), 1)
    sub = lax.broadcasted_iota(jnp.int32, (8, 128), 0)
    first_lane = lane == 0
    last_lane = lane == 127

    def exists(step):
        ok = None
        for i, s, n in zip(me, step, sizes):
            if s:
                one = i < n - 1 if s > 0 else i > 0
                ok = one if ok is None else jnp.logical_and(ok, one)
        return ok

    def at(step):
        return tuple(i + s for i, s in zip(me, step))

    def back(step):
        return tuple(-s for s in step)

    barrier = pltpu.get_barrier_semaphore()

    def greet(device):
        pl.semaphore_signal(barrier, inc=1, device_id=device, device_id_type=MESH)

    place = (me[2], me[0] * ny + me[1])
    rings = []
    for k in range(1, nz):
        rings.append((0, (me[0], me[1], lax.rem(me[2] + k, nz))))
    for k in range(1, nx * ny):
        other = lax.rem(place[1] + k, nx * ny)
        rings.append((1, (other // ny, lax.rem(other, ny), me[2])))
    for _, peer in rings:
        greet(peer)
    for step in NEAR:
        pl.when(exists(step))(functools.partial(greet, at(step)))

    loads = []
    for lt in range(2):
        cols = pl.ds(lt * 128, 128)
        loads.append(pltpu.make_async_copy(disp.at[:, :, :, cols], U.at[0:3, 2:6, lt, 8:40, :], in_sem.at[4 * lt]))
        loads.append(pltpu.make_async_copy(dens.at[:, :, cols], DN.at[:, lt], in_sem.at[4 * lt + 1]))
        loads.append(pltpu.make_async_copy(mat.at[:, :, cols], MT.at[:, lt], in_sem.at[4 * lt + 2]))
        loads.append(pltpu.make_async_copy(fix.at[:, :, cols], FX.at[:, lt], in_sem.at[4 * lt + 3]))
    for c in loads:
        c.start()

    def plane_of(step):
        return 1 - step[2]

    def clear(k, ref, comps):
        for step, row in (((0, -1, 0), 7), ((0, 1, 0), 40)):
            def fill(row=row):
                for c in range(comps):
                    for x in range(9):
                        for lt in range(2):
                            ref[c, x, lt, row : row + 1, :] = jnp.full((1, 128), OUTSIDE[c], F32)
            pl.when(jnp.logical_not(exists(step)))(fill)
        for step in TILES:
            def fill(step=step):
                TR[k, plane_of(step), step[1] + 1] = outside
            pl.when(jnp.logical_not(exists(back(step))))(fill)

    outside = jnp.where(lane % 4 == 3, -1.0, 0.0)
    for step, planes in (((-1, 0, 0), (0, 1)), ((1, 0, 0), (6, 7, 8))):
        def fill(planes=planes):
            for c in range(5):
                for x in planes:
                    for lt in range(2):
                        U[c, x, lt, 7:41, :] = jnp.full((34, 128), OUTSIDE[c], F32)
        pl.when(jnp.logical_not(exists(step)))(fill)
    for step in LINES:
        def fill(step=step):
            for i in range(3):
                LR[plane_of(step), (1 - step[0]) // 2, step[1] + 1, i] = outside[0:1]
        pl.when(jnp.logical_not(exists(back(step))))(fill)
    clear(0, U, 4)
    clear(1, FI, 3)
    clear(2, AD, 3)
    for c in loads:
        c.wait()

    for x in range(4):
        for lt in range(2):
            m = MT[x, lt]
            U[3, x + 2, lt, 8:40, :] = jnp.where(m == 1, DN[x, lt], jnp.where(m == 2, 1.0, 0.0))
            U[4, x + 2, lt, 8:40, :] = FX[x, lt].astype(F32)

    def pack(ref, comps, high, xs):
        lt, source = (1, 127) if high else (0, 0)
        parts = []
        for g in range(4):
            part = jnp.zeros((8, 128), F32)
            for c in range(comps):
                for x in xs:
                    to = 32 * g + 4 * x + c
                    v = ref[c, x, lt, 8 + 8 * g : 16 + 8 * g, :]
                    part = jnp.where(lane == to, pltpu.roll(v, (to - source) % 128, 1), part)
            parts.append(part)
        return (parts[0] + parts[1]) + (parts[2] + parts[3])

    def line(tile, x):
        out = jnp.zeros((8, 128), F32)
        mine = (lane % 32) // 4 == 7 - sub
        for i in range(8):
            out = jnp.where(jnp.logical_and(mine, sub == i), pltpu.roll(tile, (28 - 4 * i - 4 * x) % 128, 1), out)
        return jnp.sum(out, axis=0, keepdims=True)

    def spread(row, x):
        moved = pltpu.roll(jnp.broadcast_to(row, (8, 128)), 0, 1, stride=4, stride_axis=0)
        return pltpu.roll(moved, (100 + 4 * x) % 128, 1)

    def remote(src, dst, send, recv, step):
        return (step, pltpu.make_async_remote_copy(
            src_ref=src, dst_ref=dst, send_sem=send, recv_sem=recv, device_id=at(step), device_id_type=MESH))

    def sides(ref, steps, comps, planes, send, recv):
        out = []
        for i, (dx, dy) in enumerate(steps):
            (sx, tx), (sr, tr) = span(dx) if dx else (planes, planes), rows_of(dy)
            out.append(remote(ref.at[0:comps, sx, :, sr, :], ref.at[0:comps, tx, :, tr, :], send.at[i], recv.at[i], (dx, dy, 0)))
        return out

    def tiles(k, steps, send, recv):
        return [remote(TS.at[k, 1 if step[2] > 0 else 0], TR.at[k, plane_of(step), step[1] + 1], send.at[i], recv.at[i], step)
                for i, step in enumerate(steps)]

    def lines(steps, send, recv):
        out = []
        for i, step in enumerate(steps):
            planes, count, side = (slice(2, 4), 2, 0) if step[0] > 0 else (slice(0, 3), 3, 1)
            out.append(remote(LS.at[1 if step[2] > 0 else 0, planes], LR.at[plane_of(step), side, step[1] + 1, 0:count],
                              send.at[i], recv.at[i], step))
        return out

    middle = nx // 2
    own = slice(8, 40)

    def plane_copy(comps, src, dst, i, step):
        return remote(U.at[comps, src, :, own, :], U.at[comps, dst, :, own, :], xs_.at[i], xr_.at[i], step)

    wide = [plane_copy(slice(0, 3), slice(4, 6), slice(0, 2), 0, (1, 0, 0)), plane_copy(slice(0, 3), slice(2, 5), slice(6, 9), 1, (-1, 0, 0))]
    thin = [plane_copy(slice(3, 5), slice(4, 6), slice(0, 2), 2, (1, 0, 0)), plane_copy(slice(3, 5), slice(2, 4), slice(6, 8), 3, (-1, 0, 0))]
    low_side, high_side = me[0] == middle - 1, me[0] == middle

    def plain(step):
        return jnp.logical_and(exists(step), jnp.logical_not(low_side if step[0] > 0 else high_side))

    def hop(c, up, leg):
        count = 2 if up else 3
        src = U.at[c, slice(4, 6) if up else slice(2, 5), :, own, :]
        dst = U.at[c, slice(0, 2) if up else slice(6, 9), :, own, :]
        stage = ST.at[c, 0:count]
        if leg == 0:
            pair, to = (src, stage), relay_of(c, up)
        else:
            pair, to = (src if ROUTE[c] is None else stage, dst), (middle if up else middle - 1)
        i = (2 * c + (0 if up else 1)) * 2 + leg
        return pltpu.make_async_remote_copy(src_ref=pair[0], dst_ref=pair[1], send_sem=hs_.at[i], recv_sem=hr_.at[i],
                                            device_id=(to, me[1], me[2]), device_id_type=MESH)

    def relay_of(c, up):
        return ROUTE[c] if up else nx - 1 - ROUTE[c]

    crossings = [(c, up, low_side if up else high_side, high_side if up else low_side) for c in ORDER for up in (True, False)]

    def send_across():
        for c, up, here, _ in crossings:
            pl.when(here)(hop(c, up, 1 if ROUTE[c] is None else 0).start)

    def send_planes():
        for step, c in wide:
            pl.when(plain(step))(c.start)

    def relay_planes():
        for c, up, _, _ in crossings:
            if ROUTE[c] is not None:
                def forward(c=c, up=up):
                    hop(c, up, 0).wait_recv()
                    hop(c, up, 1).start()
                pl.when(me[0] == relay_of(c, up))(forward)

    def arrive_planes():
        for step, c in wide:
            pl.when(plain(back(step)))(c.wait_recv)
        for c, up, _, there in crossings:
            pl.when(there)(hop(c, up, 1).wait_recv)

    def left_planes():
        left(thin)
        for step, c in wide:
            pl.when(plain(step))(c.wait_send)
        for c, up, here, _ in crossings:
            if ROUTE[c] is None:
                pl.when(here)(hop(c, up, 1).wait_send)
            else:
                pl.when(here)(hop(c, up, 0).wait_send)
                pl.when(me[0] == relay_of(c, up))(hop(c, up, 1).wait_send)

    def along(copies):
        return [c for c in copies if c[0][0] == 0], [c for c in copies if c[0][0] != 0]

    def start(copies):
        for step, c in copies:
            pl.when(exists(step))(c.start)

    def arrive(copies):
        for step, c in copies:
            pl.when(exists(back(step)))(c.wait_recv)

    def left(copies):
        for step, c in copies:
            pl.when(exists(step))(c.wait_send)

    def merge(k, plane, with_x):
        for dy in (-1, 0, 1):
            full = TS[k, 0] if plane == 1 and dy == 0 else TR[k, plane, dy + 1]
            if with_x:
                for side, i, x in ((0, 0, 0), (0, 1, 1), (1, 0, 6), (1, 1, 7)):
                    here = jnp.logical_and(lane % 32 >= 4 * x, lane % 32 < 4 * x + 4)
                    full = jnp.where(here, spread(LR[plane, side, dy + 1, i], x), full)
                far = spread(LR[plane, 1, dy + 1, 2], 0)

            def unfold(shift):
                part = pltpu.roll(full, shift, 1) if shift else full
                if with_x:
                    part = jnp.where(jnp.logical_and(lane >= 32, lane < 36), pltpu.roll(far, (shift + 32) % 128, 1), part)
                return part

            if dy == 0:
                for g in range(4):
                    PL[plane, 8 + 8 * g : 16 + 8 * g, :] = unfold((128 - 32 * g) % 128)
            elif dy == 1:
                PL[plane, 0:8, :] = unfold(32)
            else:
                PL[plane, 40:48, :] = unfold(0)

    def sweep_z(ref, xs, lts=(0, 1), begin=7, count=5, stride=8):
        def body(g, carry):
            rows = pl.ds(begin + stride * g, 8)
            edge = PL[2, rows, :] if 1 in lts else None
            for c in range(3):
                for x in xs:
                    t1 = ref[c, x, 1, rows, :]
                    r1 = pltpu.roll(t1, 127, 1)
                    if 0 in lts:
                        t0 = ref[c, x, 0, rows, :]
                        s0 = jnp.where(last_lane, r1, pltpu.roll(t0, 127, 1))
                        PS[c, x, 0, rows, :] = s0 + t0
                        QS[c, x, 0, rows, :] = s0 - t0
                    if 1 in lts:
                        s1 = jnp.where(last_lane, pltpu.roll(edge, 127 - 4 * x - c, 1), r1)
                        PS[c, x, 1, rows, :] = s1 + t1
                        QS[c, x, 1, rows, :] = s1 - t1
            return carry
        lax.fori_loop(0, count, body, 0)

    def gradients(low, high):
        return [[high[c][0] - low[c][0] for c in range(3)], [high[c][1] + low[c][1] for c in range(3)],
                [high[c][2] + low[c][2] for c in range(3)]]

    def strain6(g):
        gx, gy, gz = g
        return gx[0], gy[1], gz[2], gy[0] + gx[1], gz[1] + gy[2], gx[2] + gz[0]

    def y_sums(x, lt, base):
        out = []
        for c in range(3):
            p0, p1 = PS[c, x, lt, pl.ds(base, 8), :], PS[c, x, lt, pl.ds(base + 1, 8), :]
            q0, q1 = QS[c, x, lt, pl.ds(base, 8), :], QS[c, x, lt, pl.ds(base + 1, 8), :]
            out.append((p0 + p1, p1 - p0, q0 + q1))
        return out

    def packed_strain():
        lo, hi = PL[0], PL[1]
        PK[0] = lo + hi
        PK[1] = hi - lo
        p0, p1, q0, q1 = PK[0, 0:40], PK[0, 1:41], PK[1, 0:40], PK[1, 1:41]
        a, b, c = p0 + p1, p1 - p0, q0 + q1
        g = [pltpu.roll(a, 124, 1) - a, pltpu.roll(b, 124, 1) + b, pltpu.roll(c, 124, 1) + c]
        return strain6([[t] + [pltpu.roll(t, 128 - i, 1) for i in (1, 2)] for t in g])

    def stiffness(d):
        return jnp.where(d < 0.0, 0.0, 0.001 + d * d * d)

    def load_terms(e, d):
        a, b, c = e[0] - e[1], e[1] - e[2], e[2] - e[0]
        q = (MU * MU / 16.0) * (2.0 * (a * a + b * b + c * c) + 3.0 * (e[3] * e[3] + e[4] * e[4] + e[5] * e[5]))
        vm = d * q
        w = vm * vm * vm
        t = (-MU * MU / 8.0 * BOOST) * (w * d)
        ts = 1.5 * t
        return q, vm, w, (t * (a - c), t * (b - a), t * (c - b), ts * e[3], ts * e[4], ts * e[5])

    def stiff_terms(e, kf):
        k = kf * (-2.0 * MU / 16.0)
        tr = (kf * (-LAM / 16.0)) * (e[0] + e[1] + e[2])
        ks = kf * (-MU / 16.0)
        return tr + k * e[0], tr + k * e[1], tr + k * e[2], ks * e[3], ks * e[4], ks * e[5]

    S_Y, D_Y = (0, 3, 5, 4, 2), (3, 1, 4)

    def x_parts(low, high):
        (sl, dl), (sh, dh) = low, high
        return [((sh[i] - sl[i]) + (dh[j] + dl[j]), sh[k] + sl[k]) for i, j, k in ((0, 3, 5), (3, 1, 4), (5, 4, 2))]

    def packed_forces(r):
        for i in range(6):
            PK[i, 0:40] = r[i]
        s = {i: PK[i, 7:39] + PK[i, 8:40] for i in S_Y}
        d = {i: PK[i, 8:40] - PK[i, 7:39] for i in D_Y}
        high = ({i: pltpu.roll(v, 124, 1) for i, v in s.items()}, {i: pltpu.roll(v, 124, 1) for i, v in d.items()})
        for c, (u, w) in enumerate(x_parts((s, d), high)):
            WP[c] = u - w

    def from_low(w0, w1, packed, x):
        r0, r1 = pltpu.roll(w0, 1, 1), pltpu.roll(w1, 1, 1)
        edge = pltpu.roll(packed, 132 - 4 * x, 1) if x > 1 else packed
        return jnp.where(first_lane, edge, r0), jnp.where(first_lane, r0, r1)

    def forces(xs, finish):
        def body(g, carry):
            base = pl.multiple_of(8 + 8 * g, 8)
            own = pl.ds(pl.multiple_of(8 * g, 8), 8)
            packed = [WP[c, own, :] for c in range(3)]

            def sums(x):
                out = []
                for lt in range(2):
                    r1 = [R6[i, x, lt, pl.ds(base, 8), :] for i in range(6)]
                    r0 = [R6[i, x, lt, pl.ds(base - 1, 8), :] for i in range(6)]
                    out.append(({i: r0[i] + r1[i] for i in S_Y}, {i: r1[i] - r0[i] for i in D_Y}))
                return out

            low = sums(xs[0] - 1)
            for x in xs:
                high = sums(x)
                p0, p1 = x_parts(low[0], high[0]), x_parts(low[1], high[1])
                for c in range(3):
                    (u0, c0), (u1, c1) = p0[c], p1[c]
                    s0, s1 = from_low(u0 - c0, u1 - c1, packed[c], x)
                    finish(c, x, 0, base, own, u0 + c0 + s0)
                    finish(c, x, 1, base, own, u1 + c1 + s1)
                low = high
            return carry
        lax.fori_loop(0, 4, body, 0)

    TS[0, 0] = pack(U, 4, False, range(2, 6))
    TS[0, 1] = pack(U, 4, True, range(2, 6))
    for z in range(2):
        for x in range(4):
            LS[z, x] = line(TS[0, z], x + 2)

    t1 = tiles(0, TILES, t1s, t1r)
    l1 = lines(LINES, l1s, l1r)
    f1, x1 = along(sides(U, [d for d in SIDES if d[1]], 4, slice(2, 6), f1s, f1r))
    t2 = tiles(1, TILES, t2s, t2r)
    f2 = sides(FI, [(0, 1), (0, -1)], 3, slice(1, 8), f2s, f2r)
    t3 = tiles(2, LAST_TILES, t3s, t3r)
    f3 = sides(AD, [(0, -1)], 3, slice(2, 7), f3s, f3r)

    block = 1
    for i, n in zip(me, sizes):
        block = block * (1 + (i > 0).astype(jnp.int32) + (i < n - 1).astype(jnp.int32))
    pl.semaphore_wait(barrier, block - 1 + len(rings))

    send_across()
    start(thin)
    start(x1)
    start(l1)
    start(t1)
    start(f1)
    send_planes()
    relay_planes()

    def power(xs, total):
        def body(g, total):
            base = pl.multiple_of(8 * g, 8)
            rows = pl.ds(base, 8)
            own = pl.ds(pl.multiple_of(jnp.maximum(8 * g - 8, 0), 8), 8)
            inside = jnp.full((8, 128), g, jnp.int32) > 0
            for lt in range(2):
                low = y_sums(xs[0], lt, base)
                for x in xs:
                    high = y_sums(x + 1, lt, base)
                    e = strain6(gradients(low, high))
                    low = high
                    q, vm, w, r = load_terms(e, jnp.maximum(U[3, x, lt, rows, :], 0.0))
                    for i in range(6):
                        R6[i, x, lt, rows, :] = r[i]
                    if 2 <= x < 6:
                        v2 = vm * vm
                        total = total + jnp.where(inside, v2 * v2, 0.0)
                        tr = (LAM / 16.0) * (e[0] + e[1] + e[2])
                        for i in range(6):
                            S0[i, x - 2, lt, own, :] = tr + (MU / 8.0) * e[i] if i < 3 else (MU / 16.0) * e[i]
                        SE[x - 2, lt, own, :] = jnp.where(MT[x - 2, lt, own, :] == 1, (0.5 * BOOST) * (w * q), 0.0)
            return total
        return lax.fori_loop(0, 5, body, total)

    def fill_stiffness(xs):
        for x in xs:
            for lt in range(2):
                KF[x, lt, 0:40, :] = stiffness(U[3, x, lt, 0:40, :])

    def packed_load():
        d = pltpu.roll(PL[0, 0:40, :], 125, 1)
        kp = stiffness(d)
        packed_forces(load_terms(packed_strain(), jnp.maximum(d, 0.0))[3])
        PK[6, 0:40] = kp
        ky = PK[6, 7:39] + PK[6, 8:40]
        WP[3] = ky + pltpu.roll(ky, 124, 1)

    def diagonal(xs):
        def body(g, carry):
            base = pl.multiple_of(8 + 8 * g, 8)
            own = pl.ds(pl.multiple_of(8 * g, 8), 8)
            packed = WP[3, own, :]

            def sums(x):
                return [KF[x, lt, pl.ds(base, 8), :] + KF[x, lt, pl.ds(base - 1, 8), :] for lt in range(2)]

            low = sums(xs[0] - 1)
            for x in xs:
                high = sums(x)
                k0, k1 = low[0] + high[0], low[1] + high[1]
                s0, s1 = from_low(k0, k1, packed, x)
                for lt, k in ((0, k0 + s0), (1, k1 + s1)):
                    fixed = U[4, x, lt, pl.ds(base, 8), :]
                    FD[x, lt, own, :] = (1.0 - fixed) / (DIAG * k + fixed)
                low = high
            return carry
        lax.fori_loop(0, 4, body, 0)

    def first_out(c, x, lt, base, own, value):
        FI[c, x, lt, pl.ds(base, 8), :] = value * FD[x, lt, own, :]

    def ring(stage):
        buf = SUM if stage == 0 else SUM2
        return [pltpu.make_async_remote_copy(
            src_ref=buf.at[place[stage]], dst_ref=buf.at[place[stage]],
            send_sem=ass.at[i], recv_sem=asr.at[i], device_id=peer, device_id_type=MESH)
            for i, (a, peer) in enumerate(rings) if a == stage]

    def send_sum(stage, value):
        (SUM if stage == 0 else SUM2)[place[stage]] = value
        for c in ring(stage):
            c.start()

    def take_sum(stage):
        for c in ring(stage):
            c.wait_recv()
        buf, n = (SUM, nz) if stage == 0 else (SUM2, nx * ny)
        value = buf[0]
        for i in range(1, n):
            value = value + buf[i]
        return value

    arrive(t1)
    arrive(f1)
    for plane in range(3):
        merge(0, plane, False)
    packed_load()
    sweep_z(U, range(2, 6))
    total = power((2, 3, 4), jnp.zeros((8, 128), F32))
    fill_stiffness(range(2, 6))
    diagonal((3, 4, 5))
    forces((3, 4), first_out)

    arrive(l1)
    arrive(x1)
    for plane in range(3):
        merge(0, plane, True)
    packed_load()
    arrive(thin)
    fill_stiffness((0, 1, 6, 7))
    diagonal((1, 2))
    diagonal((6, 7))
    arrive_planes()
    sweep_z(U, (0, 1, 6, 7, 8))
    total = power((5, 6, 7), total)
    send_sum(0, jnp.sum(total, axis=0, keepdims=True))
    power((0, 1), total)
    forces((1, 2), first_out)
    forces((5, 6, 7), first_out)
    start(f2)
    TS[1, 0] = pack(FI, 3, False, range(1, 8))
    TS[1, 1] = pack(FI, 3, True, range(1, 8))
    start(t2)

    def stiff(xs, lts, begin, count, stride):
        def body(g, carry):
            base = pl.multiple_of(begin + stride * g, 8)
            rows = pl.ds(base, 8)
            for lt in lts:
                low = y_sums(xs[0], lt, base)
                for x in xs:
                    high = y_sums(x + 1, lt, base)
                    r = stiff_terms(strain6(gradients(low, high)), KF[x, lt, rows, :])
                    low = high
                    for i in range(6):
                        R6[i, x, lt, rows, :] = r[i]
            return carry
        lax.fori_loop(0, count, body, 0)

    def packed_stiff():
        packed_forces(stiff_terms(packed_strain(), kp_ref[...]))

    def adjoint_out(c, x, lt, base, own, value):
        new = (1.0 + RELAX) * FI[c, x, lt, pl.ds(base, 8), :] - RELAX * FD[x, lt, own, :] * value
        AD[c, x, lt, pl.ds(base, 8), :] = new
        if x < 6:
            adj_out[c, x - 2, lt, own, :] = new

    kp_ref = PK.at[6, 0:40]
    sweep_z(FI, range(1, 8), (0,), 8, 4)
    stiff(range(1, 7), (0,), 8, 3, 8)
    send_sum(1, take_sum(0))
    arrive(t2)
    arrive(f2)
    for plane in range(3):
        merge(1, plane, False)
    packed_stiff()
    sweep_z(FI, range(1, 8), (1,))
    sweep_z(FI, range(1, 8), (0,), 0, 2, 40)
    stiff(range(1, 7), (0,), 0, 2, 32)
    stiff(range(1, 7), (1,), 0, 5, 8)
    forces(range(2, 7), adjoint_out)
    start(f3)
    TS[2, 0] = pack(AD, 3, False, range(2, 7))
    start(t3)

    def last(xs, lts, begin, count):
        def body(g, carry):
            base = pl.multiple_of(begin + 8 * g, 8)
            rows = pl.ds(base, 8)
            own = pl.ds(pl.multiple_of(begin - 8 + 8 * g, 8), 8)
            for lt in lts:
                low = y_sums(xs[0] + 2, lt, base)
                for x in xs:
                    high = y_sums(x + 3, lt, base)
                    e = strain6(gradients(low, high))
                    low = high
                    dot = e[0] * S0[0, x, lt, own, :]
                    for i in range(1, 6):
                        dot = dot + e[i] * S0[i, x, lt, own, :]
                    d = U[3, x + 2, lt, rows, :]
                    slope = jnp.where(MT[x, lt, own, :] == 1, 3.0 * (d * d), 0.0)
                    sens_out[x, lt, own, :] = SE[x, lt, own, :] - slope * dot
            return carry
        lax.fori_loop(0, count, body, 0)

    sweep_z(AD, range(2, 7), (0,), 8, 4)
    last((0, 1, 2, 3), (0,), 8, 3)
    arrive(t3)
    arrive(f3)
    merge(2, 2, False)
    sweep_z(AD, range(2, 7), (1,))
    sweep_z(AD, range(2, 7), (0,), 40, 1)
    last((0, 1, 2, 3), (0,), 32, 1)
    last((0, 1, 2, 3), (1,), 8, 4)
    sum_out[...] = take_sum(1)
    left_planes()
    for copies in (t1, l1, f1, x1, t2, f2, t3, f3):
        left(copies)
    for stage in range(2):
        for c in ring(stage):
            c.wait_send()


def finish_kernel(count, adj, sens, total, adj_out, sens_out):
    mean = jnp.full((8, 128), jnp.sum(total[...]) * (1.0 / count) + SHIFT, F32)
    scale = (jnp.sqrt(jnp.sqrt(jnp.sqrt(mean))) / mean * (1.0 / BOOST))[0:1]
    for x in range(4):
        for lt in range(2):
            cols = slice(128 * lt, 128 * lt + 128)
            sens_out[x, :, cols] = sens[x, lt] * scale
            for c in range(3):
                adj_out[c, x, :, cols] = adj[c, x, lt] * scale


def solution(mesh):
    sizes = tuple(mesh.shape[a] for a in ("gx", "gy", "gz"))
    peers = sizes[2] - 1 + sizes[0] * sizes[1] - 1
    count = sizes[0] * sizes[1] * sizes[2] * 4 * 32 * 256

    def per_device(displacement, density, material, fixed_mask):
        dma = pltpu.SemaphoreType.DMA
        vmem = pl.BlockSpec(memory_space=pltpu.VMEM)
        both = lambda n: [dma((n,)), dma((n,))]
        adj, sens, total = pl.pallas_call(
            functools.partial(kernel, sizes),
            out_shape=(pltpu.VMEM((3, 4, 2, 32, 128), F32), pltpu.VMEM((4, 2, 32, 128), F32), pltpu.VMEM((1, 128), F32)),
            in_specs=[pl.BlockSpec(memory_space=pl.ANY)] * 4,
            out_specs=[vmem] * 3,
            scratch_shapes=[
                pltpu.VMEM((5, 9, 2, ROWS, 128), F32),
                pltpu.VMEM((3, 9, 2, ROWS, 128), F32),
                pltpu.VMEM((3, 9, 2, ROWS, 128), F32),
                pltpu.VMEM((4, 2, 32, 128), F32),
                pltpu.VMEM((4, 2, 32, 128), jnp.int32),
                pltpu.VMEM((4, 2, 32, 128), jnp.int32),
                pltpu.VMEM((3, 9, 2, ROWS, 128), F32),
                pltpu.VMEM((3, 9, 2, ROWS, 128), F32),
                pltpu.VMEM((6, 8, 2, ROWS, 128), F32),
                pltpu.VMEM((8, 2, ROWS, 128), F32),
                pltpu.VMEM((6, 4, 2, 32, 128), F32),
                pltpu.VMEM((4, 2, 32, 128), F32),
                pltpu.VMEM((8, 2, 32, 128), F32),
                pltpu.VMEM((3, 2, 8, 128), F32),
                pltpu.VMEM((2, 4, 1, 128), F32),
                pltpu.VMEM((3, 3, 3, 8, 128), F32),
                pltpu.VMEM((3, 2, 3, 3, 1, 128), F32),
                pltpu.VMEM((3, ROWS, 128), F32),
                pltpu.VMEM((7, ROWS, 128), F32),
                pltpu.VMEM((4, 32, 128), F32),
                pltpu.VMEM((sizes[2], 1, 128), F32),
                pltpu.VMEM((sizes[0] * sizes[1], 1, 128), F32),
                pltpu.VMEM((3, 3, 2, 32, 128), F32),
                dma((8,)),
                *both(4), *both(12), *both(6), *both(8), *both(18),
                *both(2), *both(8), *both(1), *both(2),
                *both(peers),
            ],
            compiler_params=pltpu.CompilerParams(collective_id=0, has_side_effects=True),
        )(displacement, density, material, fixed_mask)
        return pl.pallas_call(
            functools.partial(finish_kernel, count),
            out_shape=(jax.ShapeDtypeStruct((3, 4, 32, 256), F32), jax.ShapeDtypeStruct((4, 32, 256), F32)),
            in_specs=[vmem] * 3,
            out_specs=[vmem] * 2,
        )(*(pltpu.with_memory_space_constraint(v, pltpu.VMEM) for v in (adj, sens, total)))

    placed = (P(None, "gx", "gy", "gz"), P("gx", "gy", "gz"), P("gx", "gy", "gz"), P("gx", "gy", "gz"))
    return jax.shard_map(per_device, mesh=mesh, in_specs=placed, out_specs=(placed[0], placed[1]), check_vma=False)
```
